256 devices in a mesh: slab: 32 (over x, y, core), cross: 8 (over z).
Axes of the slice: x: 4, y: 4, z: 8, core: 2. Of those that a mesh axis runs over, the one named last changes fastest.
Arguments:
- velocity: float32 [3, 128, 32, 128], P(None, 'slab', 'cross'), may hold values from -6 to 6
- acceleration: float32 [3, 128, 32, 128], P(None, 'slab', 'cross'), may hold values from -6 to 6
- grad_coef: float32 [3, 128, 32, 128], P(None, 'slab', 'cross'), may hold values from -6 to 6
- density_dev: float32 [128, 32, 128], P('slab', 'cross'), may hold values from -3 to 3
- self_weight: float32 [128, 32, 128], P('slab', 'cross'), may hold values from 0.5 to 4
- self_tiles: float32 [128, 32, 128, 128], P('slab', 'cross'), may hold values from -0.015625 to 0
- edge_tiles: float32 [128, 32, 4, 128, 128], P('slab', 'cross'), may hold values from -0.015625 to 0
- tile_count: int32 [128, 32], P('slab', 'cross'), may hold values from 1 to 4
- tile_offset: int32 [128, 32, 4], P('slab', 'cross'), may hold values from 0 to 3, as said below
- ghost_owner: int32 [32], P('cross'), may hold values from 0 to 3, as said below
- ghost_mirror: int32 [32, 128], P('cross'), may hold values from 0 to 127, as said below
- ghost_gain: float32 [32, 128], P('cross'), may hold values from 0.5 to 2
Outputs:
- pressure: float32 [128, 32, 128], P('slab', 'cross')
- residual: float32 [128, 32, 128], P('slab', 'cross')
The draws below stay inside these ranges and needn't reach their ends.
Inputs may be any that keep to these rules, and one draw needn't show every extreme that they name: `tile_offset`: in every block row the 4 codes are all different. `ghost_owner`: each aligned group of 4 entries is a permutation of 0 to 3. `ghost_mirror`: each row is a permutation of 0 to 127.
All inputs are finite; a program needn't handle non-finite values.
Results may differ from the reference program's by a relative error of at most 0.0003.
Values sent between devices are 32-bit elements; how exact they have to be, the bound alone decides.
No kernel may reach another device: no remote copies, remote signals or barrier semaphores. Data moves between devices by JAX's collectives and lax.ppermute only.
A program may use at most 128 MiB of HBM per device.

```python
import math
import jax
import jax.numpy as jnp
from jax import lax

BS = 128
SLOTS = 4
ITERS = 2
BC = 4
GA = 128
GC = 32


def draw_tile_offset(key, part):
    key = jax.random.fold_in(key, 101)
    scores = jax.random.randint(key, (GA, GC, SLOTS), 0, 1 << 20) * SLOTS + jnp.arange(SLOTS, dtype=jnp.int32)
    return jnp.argsort(scores, axis=-1).astype(jnp.int32)


def draw_ghost_owner(key, part):
    key = jax.random.fold_in(key, 202)
    scores = jax.random.randint(key, (GC // BC, BC), 0, 1 << 20) * BC + jnp.arange(BC, dtype=jnp.int32)
    return jnp.argsort(scores, axis=-1).astype(jnp.int32).reshape(GC)


def draw_ghost_mirror(key, part):
    key = jax.random.fold_in(key, 303)
    scores = jax.random.randint(key, (GC, BS), 0, 1 << 20) * BS + jnp.arange(BS, dtype=jnp.int32)
    return jnp.argsort(scores, axis=-1).astype(jnp.int32)


def set_ends(entries, rng, least, largest):
    extent = entries.shape
    spot = [jax.random.randint(jax.random.fold_in(rng, axis), (), 0, extent[axis]) for axis in range(len(extent))]
    entries = entries.at[tuple(spot)].set(least)
    longest = extent.index(max(extent))
    spot[longest] = (spot[longest] + 1) % extent[longest]
    return entries.at[tuple(spot)].set(largest)


def shard_levels(own_key, dims, shards, low, high):
    loudness = 1.0
    for axis_at, blocks in shards:
        heights = jax.random.uniform(jax.random.fold_in(jax.random.fold_in(own_key, 6), axis_at), (blocks,), jnp.float32, low / len(shards), high / len(shards))
        loudness = loudness * jnp.repeat(jnp.exp(heights), dims[axis_at] // blocks).reshape((-1,) + (1,) * (len(dims) - 1 - axis_at))
    return loudness


def bell_draw(key, extent, deviation, bound, shards=(), kind=jnp.bfloat16):
    values = deviation * jax.random.normal(key, extent, jnp.float32)
    if shards:
        values = values * shard_levels(key, extent, shards, -0.22, 0.18)
    return jnp.clip(values, -bound, bound).astype(kind)


def setup_inputs(seed: int = 0) -> dict:
    key_list = jax.random.split(jax.random.key(seed), 13)
    velocity = bell_draw(key_list[0], (3, GA, GC, BS), 1.0, 6.0, ((1, 32), (2, 8)), jnp.float32)
    acceleration = bell_draw(key_list[1], (3, GA, GC, BS), 1.0, 6.0, ((1, 32), (2, 8)), jnp.float32)
    grad_coef = bell_draw(key_list[2], (3, GA, GC, BS), 1.0, 6.0, ((1, 32), (2, 8)), jnp.float32)
    density_dev = bell_draw(key_list[3], (GA, GC, BS), 0.5, 3.0, ((0, 32), (1, 8)), jnp.float32)
    self_weight = jnp.clip(jnp.exp(math.log(4.0) - 2.0794415 * jax.random.uniform(key_list[4], (GA, GC, BS), jnp.float32) ** shard_levels(key_list[4], (GA, GC, BS), ((0, 32), (1, 8)), -0.2, 0.2)), 0.5, 4.0)
    self_tiles = jnp.clip(-0.015625 + 0.015625 * jax.random.uniform(key_list[5], (GA, GC, BS, BS), jnp.float32) ** shard_levels(key_list[5], (GA, GC, BS, BS), ((0, 32), (1, 8)), -0.2, 0.2), -0.015625, 0.0)
    edge_tiles = jnp.clip(-0.015625 + 0.015625 * jax.random.uniform(key_list[6], (GA, GC, SLOTS, BS, BS), jnp.float32) ** shard_levels(key_list[6], (GA, GC, SLOTS, BS, BS), ((0, 32), (1, 8)), -0.2, 0.2), -0.015625, 0.0)
    tile_count = set_ends(jax.random.randint(key_list[7], (GA, GC), 1, SLOTS + 1), jax.random.fold_in(key_list[7], 1), 1, SLOTS).astype(jnp.int32)
    tile_offset = draw_tile_offset(jax.random.fold_in(key_list[12], 71), 0)
    ghost_owner = draw_ghost_owner(jax.random.fold_in(key_list[12], 71), 0)
    ghost_mirror = draw_ghost_mirror(jax.random.fold_in(key_list[12], 71), 0)
    ghost_gain = jnp.clip(0.5 + 1.5 * jax.random.uniform(key_list[11], (GC, BS), jnp.float32) ** shard_levels(key_list[11], (GC, BS), ((0, 8),), -0.2, 0.2), 0.5, 2.0)
    return {"velocity": velocity, "acceleration": acceleration, "grad_coef": grad_coef, "density_dev": density_dev, "self_weight": self_weight, "self_tiles": self_tiles, "edge_tiles": edge_tiles, "tile_count": tile_count, "tile_offset": tile_offset, "ghost_owner": ghost_owner, "ghost_mirror": ghost_mirror, "ghost_gain": ghost_gain}


time_step = 0.5
shift_rows = (0, 1, 1, 1)
shift_cols = (1, -1, 0, 1)
highest = lax.Precision.HIGHEST


def slot_weights(tile_count, tile_offset):
    slot_count = tile_offset.shape[-1]
    live_mask = (lax.broadcasted_iota(jnp.int32, tile_offset.shape, tile_offset.ndim - 1) < tile_count[..., None]).astype(jnp.float32)
    onehot = (tile_offset[..., None] == jnp.arange(slot_count, dtype=jnp.int32)).astype(jnp.float32)
    return onehot * live_mask[..., None]


def coupling(vector_in, self_tiles, edge_tiles, weights, ghost_gain, owner_global, ghost_mirror):
    row_count, col_count, block_len = vector_in.shape
    padded = jnp.pad(vector_in, ((1, 1), (1, 1), (0, 0)))
    neighbours = jnp.stack([padded[1 + step_row:1 + step_row + row_count, 1 + step_col:1 + step_col + col_count] for step_row, step_col in zip(shift_rows, shift_cols)], axis=2)
    picked = jnp.einsum('abko,abon->abkn', weights, neighbours, precision=highest)
    result = jnp.einsum('abij,abj->abi', self_tiles, vector_in, precision=highest)
    result = result + jnp.einsum('abji,abj->abi', self_tiles, vector_in, precision=highest)
    result = result + jnp.einsum('abkij,abkj->abi', edge_tiles, picked, precision=highest)
    transposed = jnp.einsum('abkji,abj->abki', edge_tiles, vector_in, precision=highest)
    spread = jnp.einsum('abko,abkn->abon', weights, transposed, precision=highest)
    buffer = jnp.zeros((row_count + 2, col_count + 2, block_len), jnp.float32)
    for slot_index, (step_row, step_col) in enumerate(zip(shift_rows, shift_cols)):
        buffer = buffer.at[1 + step_row:1 + step_row + row_count, 1 + step_col:1 + step_col + col_count].add(spread[:, :, slot_index])
    result = result + buffer[1:row_count + 1, 1:col_count + 1]
    wall_row = vector_in[row_count - 1]
    mirrored = wall_row[owner_global[:, None], ghost_mirror]
    returned = jnp.zeros_like(wall_row).at[owner_global[:, None], ghost_mirror].add(ghost_gain * wall_row)
    return result.at[row_count - 1].add(-(ghost_gain * mirrored + returned))


def reference(velocity, acceleration, grad_coef, density_dev, self_weight, self_tiles, edge_tiles, tile_count, tile_offset, ghost_owner, ghost_mirror, ghost_gain):
    row_count, col_count, block_len = self_weight.shape
    columns = jnp.arange(col_count, dtype=jnp.int32)
    owner_global = (columns // BC) * BC + ghost_owner
    weights = slot_weights(tile_count, tile_offset)

    def couple(field):
        return coupling(field, self_tiles, edge_tiles, weights, ghost_gain, owner_global, ghost_mirror)

    ustar = velocity + time_step * acceleration
    source = density_dev / (time_step * time_step) - jnp.sum(grad_coef * ustar, axis=0) / time_step
    degree = -couple(jnp.ones_like(self_weight))
    diagonal = self_weight + degree
    fixed_point = ((owner_global == columns)[:, None] & (ghost_mirror == jnp.arange(block_len, dtype=jnp.int32)[None, :])).astype(jnp.float32)
    jacobi = diagonal + 2.0 * jnp.diagonal(self_tiles, axis1=2, axis2=3)
    jacobi = jacobi.at[row_count - 1].add(-2.0 * ghost_gain * fixed_point)
    pressure = jnp.zeros_like(source)
    residual = source
    scaled = residual / jacobi
    direction = scaled
    norm_now = jnp.sum(residual * scaled)
    for iteration in range(ITERS):
        applied = diagonal * direction + couple(direction)
        step_size = norm_now / jnp.sum(direction * applied)
        pressure = pressure + step_size * direction
        residual = residual - step_size * applied
        if iteration + 1 < ITERS:
            scaled = residual / jacobi
            norm_next = jnp.sum(residual * scaled)
            direction = scaled + (norm_next / norm_now) * direction
            norm_now = norm_next
    return pressure, residual
```

```python
import functools

import jax
import jax.numpy as jnp
from jax import lax
from jax.experimental import pallas as pl
from jax.experimental.pallas import tpu as pltpu
from jax.sharding import PartitionSpec as P

STRIDE = 8
DUMMY = 7
CODE_STEP = (1, STRIDE - 1, STRIDE, STRIDE + 1)

VMEM = pl.BlockSpec(memory_space=pltpu.VMEM)
SMEM = pl.BlockSpec(memory_space=pltpu.SMEM)
f32 = jnp.float32


def apply_tiles(
    table, mirror_ref, gain_ref, self_ref, edge_ref, p_ref, v_ref, rows, cols, size
):
    lane = lax.broadcasted_iota(jnp.int32, (size, size), 1)
    sub = lax.broadcasted_iota(jnp.int32, (size, size), 0)
    eye = lane == sub
    columns = jnp.transpose(p_ref[...])
    mirror = jnp.transpose(mirror_ref[...])
    gain = jnp.transpose(gain_ref[...])
    lanef = lane.astype(f32)
    sums = jnp.zeros((size, size), f32)
    slots = edge_ref.shape[0] // (rows * cols)
    for r in range(rows):
        for c in range(cols):
            block = r * cols + c
            at = r * STRIDE + c + 1
            down = jnp.broadcast_to(columns[:, at : at + 1], (size, size))
            tile = jnp.where(eye, 0.0, self_ref[block])
            acc = tile * p_ref[at : at + 1, :]
            v_ref[at : at + 1, :] += jnp.sum(tile * down, axis=0, keepdims=True)
            for k in range(slots):
                j = table[block * slots + k]
                tile = edge_ref[block * slots + k]
                acc += tile * p_ref[pl.ds(j, 1), :]
                v_ref[pl.ds(j, 1), :] += jnp.sum(tile * down, axis=0, keepdims=True)
            if r == rows - 1:
                owner = table[rows * cols * slots + c]
                same = jnp.broadcast_to(owner == c, (size, size))
                hit = (lanef == mirror[:, c : c + 1]) & ~(same & eye)
                tile = jnp.where(hit, gain[:, c : c + 1], 0.0)
                j = r * STRIDE + 1 + owner
                acc += tile * p_ref[pl.ds(j, 1), :]
                v_ref[pl.ds(j, 1), :] += jnp.sum(tile * down, axis=0, keepdims=True)
            sums = jnp.where(lane == at, jnp.sum(acc, axis=1, keepdims=True), sums)
    v_ref[...] += jnp.transpose(sums)[: v_ref.shape[0], :]


def pack_sides(v_ref, east_ref, west_ref, rows, cols):
    for r in range(rows + 1):
        east_ref[2 * r : 2 * r + 2, :] = v_ref[r * STRIDE + cols : r * STRIDE + cols + 2, :]
        west_ref[2 * r : 2 * r + 2, :] = v_ref[r * STRIDE : r * STRIDE + 2, :]


def first_kernel(
    rows, cols, table, vel, acc, grad, dens, weight, mirror, gain, self_ref, edge_ref, valid,
    v_out, src_out, east, west, p_ref,
):
    size = p_ref.shape[1]
    p_ref[...] = jnp.zeros_like(p_ref)
    p_ref[: valid.shape[0], :] = valid[...]
    v_out[...] = jnp.zeros_like(v_out)
    src_out[...] = jnp.zeros_like(src_out)
    east[...] = jnp.zeros_like(east)
    west[...] = jnp.zeros_like(west)
    for r in range(rows):
        lo = r * STRIDE + 1
        total = jnp.zeros((cols, size), f32)
        for d in range(3):
            total += grad[d, r] * (vel[d, r] + 0.5 * acc[d, r])
        src = dens[r] / 0.25 - total / 0.5
        src_out[lo : lo + cols, :] = src
        v_out[lo : lo + cols, :] = -weight[r]
        east[2 * (rows + 1) + r : 2 * (rows + 1) + r + 1, :] = src[cols - 1 : cols, :]
        west[2 * (rows + 1) + r : 2 * (rows + 1) + r + 1, :] = src[0:1, :]
    apply_tiles(table, mirror, gain, self_ref, edge_ref, p_ref, v_out, rows, cols, size)
    pack_sides(v_out, east, west, rows, cols)


def second_kernel(
    rows, cols, table, mirror, gain, self_ref, edge_ref, valid, total, src,
    v_out, s_out, jac_out, east, west, p_ref,
):
    size = p_ref.shape[1]
    inside = valid[...] > 0.0
    jac = jnp.where(inside, -total[...], 1.0)
    s = jnp.where(inside, src[...] / jac, 0.0)
    p_ref[...] = jnp.zeros_like(p_ref)
    p_ref[: s.shape[0], :] = s
    s_out[...] = s
    jac_out[...] = jac
    v_out[...] = jnp.zeros_like(v_out)
    east[...] = jnp.zeros_like(east)
    west[...] = jnp.zeros_like(west)
    apply_tiles(table, mirror, gain, self_ref, edge_ref, p_ref, v_out, rows, cols, size)
    pack_sides(v_out, east, west, rows, cols)


def third_kernel(
    rows, cols, table, mirror, gain, self_ref, edge_ref, valid, total, src, s_ref, jac,
    v_out, w_out, east, west, sums_out, p_ref,
):
    size = p_ref.shape[1]
    inside = valid[...] > 0.0
    u = total[...]
    w = jnp.where(inside, u / jac[...], 0.0)
    p_ref[...] = jnp.zeros_like(p_ref)
    p_ref[: w.shape[0], :] = w
    w_out[...] = w
    v_out[...] = jnp.zeros_like(v_out)
    east[...] = jnp.zeros_like(east)
    west[...] = jnp.zeros_like(west)
    apply_tiles(table, mirror, gain, self_ref, edge_ref, p_ref, v_out, rows, cols, size)
    pack_sides(v_out, east, west, rows, cols)
    at = lax.broadcasted_iota(jnp.int32, u.shape, 0)
    column = at % STRIDE
    own = (at < rows * STRIDE) & (column >= 1) & (column <= cols)
    s = s_ref[...]

    def whole(x):
        return jnp.sum(jnp.sum(x, axis=0, keepdims=True), axis=1, keepdims=True)

    sums = (
        whole(jnp.where(own, src[...] * s, 0.0)),
        whole(jnp.where(own, s * u, 0.0)),
        whole(jnp.where(own, w * u, 0.0)),
        whole(w * v_out[...]),
    )
    lane = lax.broadcasted_iota(jnp.int32, (1, size), 1)
    line = jnp.zeros((1, size), f32)
    for k, value in enumerate(sums):
        line = jnp.where(lane == k, value, line)
    sums_out[...] = jnp.broadcast_to(line, sums_out.shape)


def last_kernel(rows, cols, gathered, v, s_ref, jac_ref, w_ref, pressure, residual):
    nu = jnp.sum(gathered[...], axis=0, keepdims=True)
    nu0, nu1, nu2, nu3 = (nu[:, k : k + 1] for k in range(4))
    rho = nu1 / nu0
    a0 = 1.0 / (1.0 + rho)
    norm1 = a0 * a0 * (nu2 - rho * nu1)
    beta = norm1 / nu0
    g = a0 * rho + beta
    cross = g * g * nu1 - 2.0 * g * a0 * nu2 + a0 * a0 * nu3
    sigma = jnp.where(norm1 > 0.0, beta + cross / norm1, 0.0)
    step = 1.0 / (1.0 + sigma)
    rest = sigma * step
    ps, pw = a0 + step * g, -step * a0
    rs, rw, rv = a0 * rho * rest - step * beta, -a0 * rest - step * g, step * a0
    for r in range(rows):
        lo = r * STRIDE + 1
        s, w, jac = s_ref[lo : lo + cols, :], w_ref[lo : lo + cols, :], jac_ref[lo : lo + cols, :]
        pressure[r] = ps * s + pw * w
        residual[r] = jac * (rs * s + rw * w) + rv * v[lo : lo + cols, :]


def shift(value, axis, step):
    count = lax.axis_size(axis)
    return lax.ppermute(value, axis, [(i, (i + step) % count) for i in range(count)])


def per_device(
    velocity,
    acceleration,
    grad_coef,
    density_dev,
    self_weight,
    self_tiles,
    edge_tiles,
    tile_count,
    tile_offset,
    ghost_owner,
    ghost_mirror,
    ghost_gain,
):
    rows, cols, size = self_weight.shape
    slots = tile_offset.shape[-1]
    region = (rows + 1) * STRIDE
    side = STRIDE * pl.cdiv(2 * (rows + 1) + rows, STRIDE)
    slab, cross = lax.axis_index("slab"), lax.axis_index("cross")
    n_slab, n_cross = lax.axis_size("slab"), lax.axis_size("cross")
    has_north, has_south = slab > 0, slab < n_slab - 1
    has_west, has_east = cross > 0, cross < n_cross - 1

    here = (
        jnp.arange(rows, dtype=jnp.int32)[:, None] * STRIDE
        + jnp.arange(cols, dtype=jnp.int32)[None, :]
        + 1
    )
    step = jnp.zeros_like(tile_offset)
    for code, distance in enumerate(CODE_STEP):
        step = jnp.where(tile_offset == code, distance, step)
    live = lax.broadcasted_iota(jnp.int32, tile_offset.shape, 2) < tile_count[..., None]
    target = jnp.where(live, here[..., None] + step, DUMMY)
    table = jnp.concatenate([target.reshape(-1), ghost_owner])
    mirror = jnp.zeros((size, size), f32).at[:cols].set(ghost_mirror.astype(f32))
    gain = jnp.zeros((size, size), f32).at[:cols].set(
        jnp.where(has_south, 0.0, -ghost_gain)
    )
    at = lax.broadcasted_iota(jnp.int32, (region, size), 0)
    column = at % STRIDE
    valid = (
        (column <= cols + 1)
        & ((column > 0) | has_west)
        & ((column <= cols) | has_east)
        & ((at < rows * STRIDE) | has_south)
    ).astype(f32)
    selfs = self_tiles.reshape(rows * cols, size, size)
    edges = edge_tiles.reshape(rows * cols * slots, size, size)

    def call(kernel, shapes, scratch, *operands):
        return pl.pallas_call(
            functools.partial(kernel, rows, cols),
            out_shape=[jax.ShapeDtypeStruct(shape, f32) for shape in shapes],
            in_specs=[SMEM if x is table else VMEM for x in operands],
            out_specs=[VMEM] * len(shapes),
            scratch_shapes=[pltpu.VMEM((size, size), f32)] if scratch else [],
        )(*operands)

    def merge_sides(v, east, west):
        from_west = jnp.where(has_west, shift(east, "cross", 1), 0.0)
        from_east = jnp.where(has_east, shift(west, "cross", -1), 0.0)
        pair = (rows + 1, 2, size)
        gap = jnp.zeros(pair, f32)
        head = 2 * (rows + 1)
        parts = [from_west[:head].reshape(pair), gap, from_east[:head].reshape(pair), gap]
        return (
            v.reshape(rows + 1, STRIDE, size) + jnp.concatenate(parts, axis=1),
            from_west[head : head + rows],
            from_east[head : head + rows],
        )

    v, src, east, west = call(
        first_kernel,
        [(region, size), (region, size), (side, size), (side, size)],
        True,
        table, velocity, acceleration, grad_coef, density_dev, self_weight,
        mirror, gain, selfs, edges, valid,
    )
    total, src_west, src_east = merge_sides(v, east, west)
    src3 = src.reshape(rows + 1, STRIDE, size)
    src3 = src3.at[:rows, 0].set(src_west).at[:rows, cols + 1].set(src_east)
    from_north = shift(total[rows], "slab", 1)
    from_south = shift(jnp.concatenate([total[0], src3[0]], axis=0), "slab", -1)
    total = total.at[0].add(jnp.where(has_north, from_north, 0.0))
    total = total.at[rows].add(from_south[:STRIDE])
    src3 = src3.at[rows].set(from_south[STRIDE:])
    src = src3.reshape(region, size)

    v, s, jac, east, west = call(
        second_kernel,
        [(region, size)] * 3 + [(side, size)] * 2,
        True,
        table, mirror, gain, selfs, edges, valid, total.reshape(region, size), src,
    )
    total, _, _ = merge_sides(v, east, west)
    from_north = shift(total[rows], "slab", 1)
    from_south = shift(total[0], "slab", -1)
    total = total.at[0].add(jnp.where(has_north, from_north, 0.0))
    total = total.at[rows].add(from_south)

    v, w, east, west, sums = call(
        third_kernel,
        [(region, size)] * 2 + [(side, size)] * 2 + [(n_slab * n_cross, size)],
        True,
        table, mirror, gain, selfs, edges, valid, total.reshape(region, size), src, s, jac,
    )
    total, _, _ = merge_sides(v, east, west)
    from_north = shift(total[rows], "slab", 1)
    total = total.at[0].add(jnp.where(has_north, from_north, 0.0))
    gathered = lax.all_to_all(sums, ("slab", "cross"), 0, 0, tiled=True)

    pressure, residual = call(
        last_kernel,
        [(rows, cols, size)] * 2,
        False,
        gathered, total.reshape(region, size), s, jac, w,
    )
    return (pressure, residual)


def solution(mesh):
    in_specs = (
        P(None, "slab", "cross", None),
        P(None, "slab", "cross", None),
        P(None, "slab", "cross", None),
        P("slab", "cross", None),
        P("slab", "cross", None),
        P("slab", "cross", None, None),
        P("slab", "cross", None, None, None),
        P("slab", "cross"),
        P("slab", "cross", None),
        P("cross"),
        P("cross", None),
        P("cross", None),
    )
    out_specs = (P("slab", "cross", None), P("slab", "cross", None))
    return jax.shard_map(
        per_device, mesh=mesh, in_specs=in_specs, out_specs=out_specs, check_vma=False
    )
```

```python
import functools

import jax
import jax.numpy as jnp
from jax import lax
from jax.experimental import pallas as pl
from jax.experimental.pallas import tpu as pltpu
from jax.sharding import PartitionSpec as P

STRIDE = 8
CODE_STEP = (1, STRIDE - 1, STRIDE, STRIDE + 1)

VMEM = pl.BlockSpec(memory_space=pltpu.VMEM)
SMEM = pl.BlockSpec(memory_space=pltpu.SMEM)
ANY = pl.BlockSpec(memory_space=pl.ANY)
f32 = jnp.float32


def inside_grid(rows, cols, shape):
    slab, cross = lax.axis_index("slab"), lax.axis_index("cross")
    has_south = slab < lax.axis_size("slab") - 1
    at = lax.broadcasted_iota(jnp.int32, shape, 0)
    column = at % STRIDE
    first = jnp.where(cross > 0, 0, 1)
    last = jnp.where(cross < lax.axis_size("cross") - 1, cols + 1, cols)
    end = jnp.where(has_south, rows + 1, rows) * STRIDE
    own = (at < rows * STRIDE) & (column >= 1) & (column <= cols)
    return (column >= first) & (column <= last) & (at < end), own


class Tiles:
    def __init__(self, rows, cols, p_ref, mask, selfs, edges, ghosts):
        self.rows, self.cols, self.p_ref, self.mask = rows, cols, p_ref, mask
        self.selfs, self.edges, self.ghosts = selfs, edges, ghosts
        self.size = p_ref.shape[1]
        full = (self.size, self.size)
        self.lane = lax.broadcasted_iota(jnp.int32, full, 1)
        self.eye = self.lane == lax.broadcasted_iota(jnp.int32, full, 0)
        self.columns = jnp.transpose(p_ref[...])
        self.sums = jnp.zeros(full, f32)
        self.parts = {}

    def fold(self, product, at, factor=None):
        part = jnp.sum(product.reshape(self.size // 8, 8, self.size), axis=0)
        if factor is not None:
            part = part * factor
        self.parts[at] = self.parts[at] + part if at in self.parts else part

    def block(self, r, c):
        size, cols = self.size, self.cols
        at = r * STRIDE + c + 1
        down = jnp.broadcast_to(self.columns[:, at : at + 1], (size, size))
        tile = jnp.where(self.eye, 0.0, self.selfs[r * cols + c])
        acc = tile * self.p_ref[at : at + 1, :]
        self.fold(tile * down, at)
        for code, distance in enumerate(CODE_STEP):
            slot = (r * cols + c) * len(CODE_STEP) + code
            live = self.mask[slot : slot + 1, :]
            j = at + distance
            tile = self.edges[slot]
            acc += tile * (self.p_ref[j : j + 1, :] * live)
            self.fold(tile * down, j, live)
        if r == self.rows - 1:
            tile = self.ghosts[c]
            base = self.rows * cols * len(CODE_STEP) + c * cols
            field = jnp.zeros((1, size), f32)
            for o in range(cols):
                j = r * STRIDE + 1 + o
                field += self.p_ref[j : j + 1, :] * self.mask[base + o : base + o + 1, :]
            acc += tile * field
            part = jnp.sum((tile * down).reshape(size // 8, 8, size), axis=0)
            for o in range(cols):
                j = r * STRIDE + 1 + o
                self.parts[j] += part * self.mask[base + o : base + o + 1, :]
        self.sums = jnp.where(self.lane == at, jnp.sum(acc, axis=1, keepdims=True), self.sums)

    def store(self, v_ref):
        v_ref[...] += jnp.transpose(self.sums)[: v_ref.shape[0], :]
        for at, part in self.parts.items():
            v_ref[at : at + 1, :] += jnp.sum(part, axis=0, keepdims=True)


def pack_sides(v_ref, east_ref, west_ref, rows, cols):
    for r in range(rows + 1):
        east_ref[2 * r : 2 * r + 2, :] = v_ref[r * STRIDE + cols : r * STRIDE + cols + 2, :]
        west_ref[2 * r : 2 * r + 2, :] = v_ref[r * STRIDE : r * STRIDE + 2, :]


def first_kernel(
    rows, cols, count, offset, owner, mirror, gain, vel, acc, grad, dens, weight,
    self_hbm, edge_hbm,
    v_out, src_out, east, west, mask, selfs, edges, ghosts, p_ref, self_sem, edge_sem,
):
    size = p_ref.shape[1]
    slots = len(CODE_STEP)
    for r in range(rows):
        part = pl.ds(r * cols, cols)
        pltpu.make_async_copy(self_hbm.at[part], selfs.at[part], self_sem.at[r]).start()
        for c in range(cols):
            for k in range(slots):
                slot = (r * cols + c) * slots + k
                place = (r * cols + c) * slots + offset[r, c, k]
                pltpu.make_async_copy(
                    edge_hbm.at[slot], edges.at[place], edge_sem.at[r]
                ).start()
                live = jnp.where(k < count[r, c], 1.0, 0.0)
                mask[pl.ds(place, 1), :] = jnp.full((1, size), live, f32)
    base = rows * cols * slots
    for c in range(cols):
        for o in range(cols):
            same = jnp.where(owner[c] == o, 1.0, 0.0)
            mask[base + c * cols + o : base + c * cols + o + 1, :] = jnp.full((1, size), same, f32)

    inside, _ = inside_grid(rows, cols, v_out.shape)
    p_ref[...] = jnp.zeros_like(p_ref)
    p_ref[: v_out.shape[0], :] = jnp.where(inside, 1.0, 0.0)
    v_out[...] = jnp.zeros_like(v_out)
    src_out[...] = jnp.zeros_like(src_out)
    for r in range(rows):
        lo = r * STRIDE + 1
        total = jnp.zeros((cols, size), f32)
        for d in range(3):
            total += grad[d, r] * (vel[d, r] + 0.5 * acc[d, r])
        src = dens[r] / 0.25 - total / 0.5
        src_out[lo : lo + cols, :] = src
        v_out[lo : lo + cols, :] = -weight[r]
        head = 2 * (rows + 1) + r
        east[head : head + 1, :] = src[cols - 1 : cols, :]
        west[head : head + 1, :] = src[0:1, :]
    for side in (east, west):
        for row in range(2 * (rows + 1) + rows, side.shape[0]):
            side[row : row + 1, :] = jnp.zeros((1, size), f32)

    on_wall = lax.axis_index("slab") == lax.axis_size("slab") - 1
    pad = jnp.zeros((size - cols, size), f32)
    mirrors = jnp.transpose(jnp.concatenate([mirror[...].astype(f32), pad], axis=0))
    gains = jnp.transpose(
        jnp.concatenate([gain[...] * jnp.where(on_wall, -1.0, 0.0), pad], axis=0)
    )
    lane = lax.broadcasted_iota(jnp.int32, (size, size), 1)
    sub = lax.broadcasted_iota(jnp.int32, (size, size), 0)
    lanef = lane.astype(f32)
    for c in range(cols):
        hit = lanef == mirrors[:, c : c + 1]
        tile = jnp.where(hit, gains[:, c : c + 1], 0.0)
        other = jnp.where(owner[c] == c, 0.0, 1.0)
        ghosts[c] = jnp.where(lane == sub, tile * other, tile)

    tiles = Tiles(rows, cols, p_ref, mask, selfs, edges, ghosts)
    for r in range(rows):
        part = pl.ds(r * cols, cols)
        pltpu.make_async_copy(self_hbm.at[part], selfs.at[part], self_sem.at[r]).wait()
        part = pl.ds(r * cols * slots, cols * slots)
        pltpu.make_async_copy(edge_hbm.at[part], edges.at[part], edge_sem.at[r]).wait()
        for c in range(cols):
            tiles.block(r, c)
    tiles.store(v_out)
    pack_sides(v_out, east, west, rows, cols)


def add_rims(rows, total, from_north, from_south, out):
    has_north = lax.axis_index("slab") > 0
    out[...] = total[...]
    out[:STRIDE, :] += jnp.where(has_north, from_north[...], 0.0)
    if from_south is not None:
        out[rows * STRIDE :, :] += from_south[:STRIDE, :]


def second_kernel(
    rows, cols, mask, selfs, edges, ghosts, total, src, from_north, from_south,
    v_out, s_out, jac_out, east, west, p_ref,
):
    inside, _ = inside_grid(rows, cols, v_out.shape)
    add_rims(rows, total, from_north, from_south, jac_out)
    s_out[...] = src[...]
    s_out[rows * STRIDE :, :] = from_south[STRIDE:, :]
    jac = jnp.where(inside, -jac_out[...], 1.0)
    s = jnp.where(inside, s_out[...] / jac, 0.0)
    p_ref[...] = jnp.zeros_like(p_ref)
    p_ref[: s.shape[0], :] = s
    s_out[...] = s
    jac_out[...] = jac
    v_out[...] = jnp.zeros_like(v_out)
    tiles = Tiles(rows, cols, p_ref, mask, selfs, edges, ghosts)
    for r in range(rows):
        for c in range(cols):
            tiles.block(r, c)
    tiles.store(v_out)
    for side in (east, west):
        side[...] = jnp.zeros_like(side)
    pack_sides(v_out, east, west, rows, cols)


def third_kernel(
    rows, cols, mask, selfs, edges, ghosts, total, src, s_ref, jac, from_north, from_south,
    v_out, w_out, east, west, sums_out, p_ref,
):
    size = p_ref.shape[1]
    inside, own = inside_grid(rows, cols, v_out.shape)
    add_rims(rows, total, from_north, from_south, w_out)
    u = w_out[...]
    w = jnp.where(inside, u / jac[...], 0.0)
    p_ref[...] = jnp.zeros_like(p_ref)
    p_ref[: w.shape[0], :] = w
    w_out[...] = w
    v_out[...] = jnp.zeros_like(v_out)
    tiles = Tiles(rows, cols, p_ref, mask, selfs, edges, ghosts)
    for r in range(rows):
        for c in range(cols):
            tiles.block(r, c)
    tiles.store(v_out)
    for side in (east, west):
        side[...] = jnp.zeros_like(side)
    pack_sides(v_out, east, west, rows, cols)
    s = s_ref[...]

    def whole(x):
        return jnp.sum(jnp.sum(x, axis=0, keepdims=True), axis=1, keepdims=True)

    sums = (
        whole(jnp.where(own, src[...] * s, 0.0)),
        whole(jnp.where(own, s * u, 0.0)),
        whole(jnp.where(own, w * u, 0.0)),
        whole(w * v_out[...]),
    )
    lane = lax.broadcasted_iota(jnp.int32, (1, size), 1)
    line = jnp.zeros((1, size), f32)
    for k, value in enumerate(sums):
        line = jnp.where(lane == k, value, line)
    sums_out[...] = jnp.broadcast_to(line, sums_out.shape)


def merge_kernel(rows, cols, with_src, with_north, *refs):
    refs = list(refs)
    v, from_west, from_east = refs[:3]
    total, south = refs[3 + with_src : 5 + with_src]
    has_west = lax.axis_index("cross") > 0
    has_east = lax.axis_index("cross") < lax.axis_size("cross") - 1
    total[...] = v[...]
    for r in range(rows + 1):
        lo = r * STRIDE
        total[lo : lo + 2, :] += jnp.where(has_west, from_west[2 * r : 2 * r + 2, :], 0.0)
        lo += cols
        total[lo : lo + 2, :] += jnp.where(has_east, from_east[2 * r : 2 * r + 2, :], 0.0)
    south[...] = total[rows * STRIDE :, :]
    if with_north:
        north = refs[5 + with_src]
        north[:STRIDE, :] = total[:STRIDE, :]
    if with_src:
        src, src_out = refs[3], refs[7]
        src_out[...] = src[...]
        for r in range(rows):
            lo, head = r * STRIDE, 2 * (rows + 1) + r
            src_out[lo : lo + 1, :] = from_west[head : head + 1, :]
            src_out[lo + cols + 1 : lo + cols + 2, :] = from_east[head : head + 1, :]
        north[STRIDE:, :] = src_out[:STRIDE, :]


def last_kernel(rows, cols, gathered, total, from_north, s_ref, jac_ref, w_ref, pressure, residual, v):
    add_rims(rows, total, from_north, None, v)
    nu = jnp.sum(gathered[...], axis=0, keepdims=True)
    nu0, nu1, nu2, nu3 = (nu[:, k : k + 1] for k in range(4))
    rho = nu1 / nu0
    a0 = 1.0 / (1.0 + rho)
    norm1 = a0 * a0 * (nu2 - rho * nu1)
    beta = norm1 / nu0
    g = a0 * rho + beta
    cross = g * g * nu1 - 2.0 * g * a0 * nu2 + a0 * a0 * nu3
    sigma = jnp.where(norm1 > 0.0, beta + cross / norm1, 0.0)
    step = 1.0 / (1.0 + sigma)
    rest = sigma * step
    ps, pw = a0 + step * g, -step * a0
    rs, rw, rv = a0 * rho * rest - step * beta, -a0 * rest - step * g, step * a0
    for r in range(rows):
        lo = r * STRIDE + 1
        s, w, jac = s_ref[lo : lo + cols, :], w_ref[lo : lo + cols, :], jac_ref[lo : lo + cols, :]
        pressure[r] = ps * s + pw * w
        residual[r] = jac * (rs * s + rw * w) + rv * v[lo : lo + cols, :]


def shift(value, axis, step):
    count = lax.axis_size(axis)
    return lax.ppermute(value, axis, [(i, (i + step) % count) for i in range(count)])


def per_device(
    velocity,
    acceleration,
    grad_coef,
    density_dev,
    self_weight,
    self_tiles,
    edge_tiles,
    tile_count,
    tile_offset,
    ghost_owner,
    ghost_mirror,
    ghost_gain,
):
    rows, cols, size = self_weight.shape
    slots = tile_offset.shape[-1]
    region = ((rows + 1) * STRIDE, size)
    side = (STRIDE * pl.cdiv(2 * (rows + 1) + rows, STRIDE), size)
    line = (STRIDE, size)
    peers = lax.axis_size("slab") * lax.axis_size("cross")

    def call(kernel, shapes, specs, operands, scratch=(), extra=(), limit=2):
        return pl.pallas_call(
            functools.partial(kernel, rows, cols, *extra),
            out_shape=[pltpu.VMEM(shape, f32) for shape in shapes],
            in_specs=specs,
            out_specs=[VMEM] * len(shapes),
            scratch_shapes=list(scratch),
            compiler_params=pltpu.CompilerParams(vmem_limit_bytes=limit << 20),
        )(*operands)

    def merge(v, east, west, src=None, north=True):
        operands = [v, shift(east, "cross", 1), shift(west, "cross", -1)]
        shapes = [region, line]
        if src is not None:
            operands.append(src)
            shapes += [(2 * STRIDE, size), region]
        elif north:
            shapes.append(line)
        return call(
            merge_kernel, shapes, [VMEM] * len(operands), operands,
            extra=(src is not None, north),
        )

    field = pltpu.VMEM((size, size), f32)
    v, src, east, west, mask, selfs, edges, ghosts = call(
        first_kernel,
        [
            region, region, side, side, (rows * cols * slots + cols * cols, size),
            (rows * cols, size, size), (rows * cols * slots, size, size), (cols, size, size),
        ],
        [SMEM] * 3 + [VMEM] * 7 + [ANY] * 2,
        [
            tile_count, tile_offset, ghost_owner, ghost_mirror, ghost_gain,
            velocity, acceleration, grad_coef, density_dev, self_weight,
            self_tiles.reshape(rows * cols, size, size),
            edge_tiles.reshape(rows * cols * slots, size, size),
        ],
        [field, pltpu.SemaphoreType.DMA((rows,)), pltpu.SemaphoreType.DMA((rows,))],
        limit=10,
    )
    matrix = [mask, selfs, edges, ghosts]
    total, south, north, src = merge(v, east, west, src)
    from_north, from_south = shift(south, "slab", 1), shift(north, "slab", -1)

    operands = matrix + [total, src, from_north, from_south]
    v, s, jac, east, west = call(
        second_kernel, [region] * 3 + [side] * 2, [VMEM] * len(operands), operands, [field]
    )
    total, south, north = merge(v, east, west)
    from_north, from_south = shift(south, "slab", 1), shift(north, "slab", -1)

    operands = matrix + [total, src, s, jac, from_north, from_south]
    v, w, east, west, sums = call(
        third_kernel,
        [region] * 2 + [side] * 2 + [(peers, size)],
        [VMEM] * len(operands), operands, [field],
    )
    gathered = lax.all_to_all(sums, ("slab", "cross"), 0, 0, tiled=True)
    total, south = merge(v, east, west, north=False)
    from_north = shift(south, "slab", 1)

    return tuple(
        pl.pallas_call(
            functools.partial(last_kernel, rows, cols),
            out_shape=[jax.ShapeDtypeStruct((rows, cols, size), f32)] * 2,
            in_specs=[VMEM] * 6,
            out_specs=[VMEM] * 2,
            scratch_shapes=[pltpu.VMEM(region, f32)],
            compiler_params=pltpu.CompilerParams(vmem_limit_bytes=2 << 20),
        )(gathered, total, from_north, s, jac, w)
    )


def solution(mesh):
    in_specs = (
        P(None, "slab", "cross", None),
        P(None, "slab", "cross", None),
        P(None, "slab", "cross", None),
        P("slab", "cross", None),
        P("slab", "cross", None),
        P("slab", "cross", None, None),
        P("slab", "cross", None, None, None),
        P("slab", "cross"),
        P("slab", "cross", None),
        P("cross"),
        P("cross", None),
        P("cross", None),
    )
    out_specs = (P("slab", "cross", None), P("slab", "cross", None))
    return jax.shard_map(
        per_device, mesh=mesh, in_specs=in_specs, out_specs=out_specs, check_vma=False
    )
```

```python
import functools

import jax
import jax.numpy as jnp
from jax import lax
from jax.experimental import pallas as pl
from jax.experimental.pallas import tpu as pltpu
from jax.sharding import PartitionSpec as P

STRIDE = 8
CODE_STEP = (1, STRIDE - 1, STRIDE, STRIDE + 1)

VMEM = pl.BlockSpec(memory_space=pltpu.VMEM)
HBM = pl.BlockSpec(memory_space=pltpu.HBM)
f32 = jnp.float32


def inside_grid(rows, cols, shape):
    slab, cross = lax.axis_index("slab"), lax.axis_index("cross")
    has_south = slab < lax.axis_size("slab") - 1
    at = lax.broadcasted_iota(jnp.int32, shape, 0)
    column = at % STRIDE
    first = jnp.where(cross > 0, 0, 1)
    last = jnp.where(cross < lax.axis_size("cross") - 1, cols + 1, cols)
    end = jnp.where(has_south, rows + 1, rows) * STRIDE
    own = (at < rows * STRIDE) & (column >= 1) & (column <= cols)
    return (column >= first) & (column <= last) & (at < end), own


class Tiles:
    def __init__(self, rows, cols, p_ref, mask, selfs, edges, ghosts):
        self.rows, self.cols, self.p_ref, self.mask = rows, cols, p_ref, mask
        self.selfs, self.edges, self.ghosts = selfs, edges, ghosts
        self.size = p_ref.shape[1]
        full = (self.size, self.size)
        self.lane = lax.broadcasted_iota(jnp.int32, full, 1)
        self.eye = self.lane == lax.broadcasted_iota(jnp.int32, full, 0)
        self.columns = jnp.transpose(p_ref[...])
        self.sums = jnp.zeros(full, f32)
        self.parts = {}

    def fold(self, product, at, factor=None):
        part = jnp.sum(product.reshape(self.size // 8, 8, self.size), axis=0)
        if factor is not None:
            part = part * factor
        self.parts[at] = self.parts[at] + part if at in self.parts else part

    def block(self, r, c):
        size, cols = self.size, self.cols
        at = r * STRIDE + c + 1
        down = jnp.broadcast_to(self.columns[:, at : at + 1], (size, size))
        tile = jnp.where(self.eye, 0.0, self.selfs[r * cols + c])
        acc = tile * self.p_ref[at : at + 1, :]
        self.fold(tile * down, at)
        for code, distance in enumerate(CODE_STEP):
            slot = (r * cols + c) * len(CODE_STEP) + code
            live = self.mask[slot : slot + 1, :]
            j = at + distance
            tile = self.edges[slot]
            acc += tile * (self.p_ref[j : j + 1, :] * live)
            self.fold(tile * down, j, live)
        if r == self.rows - 1:
            tile = self.ghosts[c]
            base = self.rows * cols * len(CODE_STEP) + c * cols
            field = jnp.zeros((1, size), f32)
            for o in range(cols):
                j = r * STRIDE + 1 + o
                field += self.p_ref[j : j + 1, :] * self.mask[base + o : base + o + 1, :]
            acc += tile * field
            part = jnp.sum((tile * down).reshape(size // 8, 8, size), axis=0)
            for o in range(cols):
                j = r * STRIDE + 1 + o
                self.parts[j] += part * self.mask[base + o : base + o + 1, :]
        self.sums = jnp.where(self.lane == at, jnp.sum(acc, axis=1, keepdims=True), self.sums)

    def store(self, v_ref):
        v_ref[...] += jnp.transpose(self.sums)[: v_ref.shape[0], :]
        for at, part in self.parts.items():
            v_ref[at : at + 1, :] += jnp.sum(part, axis=0, keepdims=True)


def on_even(axis):
    return lax.axis_index(axis) % 2 == 0


def pack_sides(v_ref, first, second, rows, cols):
    even = on_even("cross")
    for r in range(rows + 1):
        east = v_ref[r * STRIDE + cols : r * STRIDE + cols + 2, :]
        west = v_ref[r * STRIDE : r * STRIDE + 2, :]
        first[2 * r : 2 * r + 2, :] = jnp.where(even, east, west)
        second[2 * r : 2 * r + 2, :] = jnp.where(even, west, east)


def first_kernel(rows, cols, *refs):
    inputs, refs = refs[:12], refs[12:]
    (v_out, src_out, first, second, mask, selfs, edges, ghosts), refs = refs[:8], refs[8:]
    staged, (p_ref, small_sem, self_sem, edge_sem) = refs[:10], refs[10:]
    self_hbm, edge_hbm = inputs[10:]
    size = p_ref.shape[1]
    slots = len(CODE_STEP)
    small = [
        pltpu.make_async_copy(hbm, here, small_sem.at[k])
        for k, (hbm, here) in enumerate(zip(inputs[:10], staged))
    ]
    for copy in small:
        copy.start()
    for r in range(rows):
        part = pl.ds(r * cols, cols)
        pltpu.make_async_copy(self_hbm.at[part], selfs.at[part], self_sem.at[r]).start()
    count, offset, owner, mirror, gain, vel, acc, grad, dens, weight = staged
    for copy in small[:3]:
        copy.wait()
    for r in range(rows):
        for c in range(cols):
            for k in range(slots):
                slot = (r * cols + c) * slots + k
                place = (r * cols + c) * slots + offset[r, c, k]
                pltpu.make_async_copy(
                    edge_hbm.at[slot], edges.at[place], edge_sem.at[r]
                ).start()
    for r in range(rows):
        for c in range(cols):
            for k in range(slots):
                place = (r * cols + c) * slots + offset[r, c, k]
                live = jnp.where(k < count[r, c], 1.0, 0.0)
                mask[pl.ds(place, 1), :] = jnp.full((1, size), live, f32)
    base = rows * cols * slots
    for c in range(cols):
        for o in range(cols):
            same = jnp.where(owner[c] == o, 1.0, 0.0)
            mask[base + c * cols + o : base + c * cols + o + 1, :] = jnp.full((1, size), same, f32)
    for copy in small[3:]:
        copy.wait()

    inside, _ = inside_grid(rows, cols, v_out.shape)
    p_ref[...] = jnp.zeros_like(p_ref)
    p_ref[: v_out.shape[0], :] = jnp.where(inside, 1.0, 0.0)
    v_out[...] = jnp.zeros_like(v_out)
    src_out[...] = jnp.zeros_like(src_out)
    even = on_even("cross")
    for r in range(rows):
        lo = r * STRIDE + 1
        total = jnp.zeros((cols, size), f32)
        for d in range(3):
            total += grad[d, r] * (vel[d, r] + 0.5 * acc[d, r])
        src = dens[r] / 0.25 - total / 0.5
        src_out[lo : lo + cols, :] = src
        v_out[lo : lo + cols, :] = -weight[r]
        head = 2 * (rows + 1) + r
        east, west = src[cols - 1 : cols, :], src[0:1, :]
        first[head : head + 1, :] = jnp.where(even, east, west)
        second[head : head + 1, :] = jnp.where(even, west, east)
    for side in (first, second):
        for row in range(2 * (rows + 1) + rows, side.shape[0]):
            side[row : row + 1, :] = jnp.zeros((1, size), f32)

    on_wall = lax.axis_index("slab") == lax.axis_size("slab") - 1
    pad = jnp.zeros((size - cols, size), f32)
    mirrors = jnp.transpose(jnp.concatenate([mirror[...].astype(f32), pad], axis=0))
    gains = jnp.transpose(
        jnp.concatenate([gain[...] * jnp.where(on_wall, -1.0, 0.0), pad], axis=0)
    )
    lane = lax.broadcasted_iota(jnp.int32, (size, size), 1)
    sub = lax.broadcasted_iota(jnp.int32, (size, size), 0)
    lanef = lane.astype(f32)
    for c in range(cols):
        hit = lanef == mirrors[:, c : c + 1]
        tile = jnp.where(hit, gains[:, c : c + 1], 0.0)
        other = jnp.where(owner[c] == c, 0.0, 1.0)
        ghosts[c] = jnp.where(lane == sub, tile * other, tile)

    tiles = Tiles(rows, cols, p_ref, mask, selfs, edges, ghosts)
    for r in range(rows):
        part = pl.ds(r * cols, cols)
        pltpu.make_async_copy(self_hbm.at[part], selfs.at[part], self_sem.at[r]).wait()
        part = pl.ds(r * cols * slots, cols * slots)
        pltpu.make_async_copy(edge_hbm.at[part], edges.at[part], edge_sem.at[r]).wait()
        for c in range(cols):
            tiles.block(r, c)
    tiles.store(v_out)
    pack_sides(v_out, first, second, rows, cols)


def add_rims(rows, total, first, second, out):
    even = on_even("slab")
    has_north = lax.axis_index("slab") > 0
    out[...] = total[...]
    north = jnp.where(even, second[:STRIDE, :], first[:STRIDE, :])
    out[:STRIDE, :] += jnp.where(has_north, north, 0.0)
    out[rows * STRIDE :, :] += jnp.where(even, first[:STRIDE, :], second[:STRIDE, :])


def second_kernel(
    rows, cols, mask, selfs, edges, ghosts, total, src, rim1, rim2,
    v_out, s_out, jac_out, side1, side2, p_ref,
):
    inside, _ = inside_grid(rows, cols, v_out.shape)
    add_rims(rows, total, rim1, rim2, jac_out)
    s_out[...] = src[...]
    s_out[rows * STRIDE :, :] = jnp.where(
        on_even("slab"), rim1[STRIDE:, :], rim2[STRIDE:, :]
    )
    jac = jnp.where(inside, -jac_out[...], 1.0)
    s = jnp.where(inside, s_out[...] / jac, 0.0)
    p_ref[...] = jnp.zeros_like(p_ref)
    p_ref[: s.shape[0], :] = s
    s_out[...] = s
    jac_out[...] = jac
    v_out[...] = jnp.zeros_like(v_out)
    tiles = Tiles(rows, cols, p_ref, mask, selfs, edges, ghosts)
    for r in range(rows):
        for c in range(cols):
            tiles.block(r, c)
    tiles.store(v_out)
    for side in (side1, side2):
        side[...] = jnp.zeros_like(side)
    pack_sides(v_out, side1, side2, rows, cols)


def third_kernel(
    rows, cols, mask, selfs, edges, ghosts, total, src, s_ref, jac, rim1, rim2,
    v_out, w_out, side1, side2, sums_out, p_ref,
):
    size = p_ref.shape[1]
    inside, own = inside_grid(rows, cols, v_out.shape)
    add_rims(rows, total, rim1, rim2, w_out)
    u = w_out[...]
    w = jnp.where(inside, u / jac[...], 0.0)
    p_ref[...] = jnp.zeros_like(p_ref)
    p_ref[: w.shape[0], :] = w
    w_out[...] = w
    v_out[...] = jnp.zeros_like(v_out)
    tiles = Tiles(rows, cols, p_ref, mask, selfs, edges, ghosts)
    for r in range(rows):
        for c in range(cols):
            tiles.block(r, c)
    tiles.store(v_out)
    for side in (side1, side2):
        side[...] = jnp.zeros_like(side)
    pack_sides(v_out, side1, side2, rows, cols)
    s = s_ref[...]

    def whole(x):
        return jnp.sum(jnp.sum(x, axis=0, keepdims=True), axis=1, keepdims=True)

    sums = (
        whole(jnp.where(own, src[...] * s, 0.0)),
        whole(jnp.where(own, s * u, 0.0)),
        whole(jnp.where(own, w * u, 0.0)),
        whole(w * v_out[...]),
    )
    lane = lax.broadcasted_iota(jnp.int32, (1, size), 1)
    line = jnp.zeros((1, size), f32)
    for k, value in enumerate(sums):
        line = jnp.where(lane == k, value, line)
    sums_out[...] = jnp.broadcast_to(line, sums_out.shape)


def merge_kernel(rows, cols, with_src, *refs):
    v, side1, side2 = refs[:3]
    total, first, second = refs[3 + with_src : 6 + with_src]
    even = on_even("cross")
    has_west = lax.axis_index("cross") > 0
    has_east = lax.axis_index("cross") < lax.axis_size("cross") - 1
    west = jnp.where(even, side2[...], side1[...])
    east = jnp.where(even, side1[...], side2[...])
    west = jnp.where(has_west, west, 0.0)
    east = jnp.where(has_east, east, 0.0)
    total[...] = v[...]
    for r in range(rows + 1):
        lo = r * STRIDE
        total[lo : lo + 2, :] += west[2 * r : 2 * r + 2, :]
        total[lo + cols : lo + cols + 2, :] += east[2 * r : 2 * r + 2, :]
    top, bottom = total[:STRIDE, :], total[rows * STRIDE :, :]
    even = on_even("slab")
    first[:STRIDE, :] = jnp.where(even, bottom, top)
    second[:STRIDE, :] = jnp.where(even, top, bottom)
    if with_src:
        src, src_out = refs[3], refs[7]
        src_out[...] = src[...]
        for r in range(rows):
            lo, head = r * STRIDE, 2 * (rows + 1) + r
            src_out[lo : lo + 1, :] = west[head : head + 1, :]
            src_out[lo + cols + 1 : lo + cols + 2, :] = east[head : head + 1, :]
        for out in (first, second):
            out[STRIDE:, :] = src_out[:STRIDE, :]


def last_kernel(
    rows, cols, gathered, total, rim1, rim2, s_ref, jac_ref, w_ref, pressure, residual, v
):
    add_rims(rows, total, rim1, rim2, v)
    nu = jnp.sum(gathered[...], axis=0, keepdims=True)
    nu0, nu1, nu2, nu3 = (nu[:, k : k + 1] for k in range(4))
    rho = nu1 / nu0
    a0 = 1.0 / (1.0 + rho)
    norm1 = a0 * a0 * (nu2 - rho * nu1)
    beta = norm1 / nu0
    g = a0 * rho + beta
    cross = g * g * nu1 - 2.0 * g * a0 * nu2 + a0 * a0 * nu3
    sigma = jnp.where(norm1 > 0.0, beta + cross / norm1, 0.0)
    step = 1.0 / (1.0 + sigma)
    rest = sigma * step
    ps, pw = a0 + step * g, -step * a0
    rs, rw, rv = a0 * rho * rest - step * beta, -a0 * rest - step * g, step * a0
    for r in range(rows):
        lo = r * STRIDE + 1
        s, w, jac = s_ref[lo : lo + cols, :], w_ref[lo : lo + cols, :], jac_ref[lo : lo + cols, :]
        pressure[r] = ps * s + pw * w
        residual[r] = jac * (rs * s + rw * w) + rv * v[lo : lo + cols, :]


def swap(value, second, axis):
    slabs, crosses = lax.axis_size("slab"), lax.axis_size("cross")
    pairs = []
    for a in range(slabs):
        for c in range(crosses):
            if axis == "cross":
                to = (a, (((c + 1) ^ 1) - 1) % crosses if second else c ^ 1)
            elif not second:
                to = (a ^ 1, c)
            elif 0 < a < slabs - 1:
                to = (((a + 1) ^ 1) - 1, c)
            else:
                to = (a, c ^ 1)
            pairs.append((a * crosses + c, to[0] * crosses + to[1]))
    return lax.ppermute(value, ("slab", "cross"), pairs)


def per_device(
    velocity,
    acceleration,
    grad_coef,
    density_dev,
    self_weight,
    self_tiles,
    edge_tiles,
    tile_count,
    tile_offset,
    ghost_owner,
    ghost_mirror,
    ghost_gain,
):
    rows, cols, size = self_weight.shape
    slots = tile_offset.shape[-1]
    region = ((rows + 1) * STRIDE, size)
    side = (STRIDE * pl.cdiv(2 * (rows + 1) + rows, STRIDE), size)
    line = (STRIDE, size)
    peers = lax.axis_size("slab") * lax.axis_size("cross")

    def call(kernel, shapes, specs, operands, scratch=(), extra=(), limit=2):
        return pl.pallas_call(
            functools.partial(kernel, rows, cols, *extra),
            out_shape=[pltpu.VMEM(shape, f32) for shape in shapes],
            in_specs=specs,
            out_specs=[VMEM] * len(shapes),
            scratch_shapes=list(scratch),
            compiler_params=pltpu.CompilerParams(vmem_limit_bytes=limit << 20),
        )(*operands)

    def exchange(v, first, second, src=None):
        operands = [v, swap(first, False, "cross"), swap(second, True, "cross")]
        shapes = [region, line, line]
        if src is not None:
            operands.append(src)
            shapes = [region, (2 * STRIDE, size), (2 * STRIDE, size), region]
        total, first, second, *rest = call(
            merge_kernel, shapes, [VMEM] * len(operands), operands, extra=(src is not None,)
        )
        return [total, *rest, swap(first, False, "slab"), swap(second, True, "slab")]

    field = pltpu.VMEM((size, size), f32)
    small = [
        tile_count, tile_offset, ghost_owner, ghost_mirror, ghost_gain,
        velocity, acceleration, grad_coef, density_dev, self_weight,
    ]
    staged = [
        (pltpu.SMEM if k < 3 else pltpu.VMEM)(x.shape, x.dtype) for k, x in enumerate(small)
    ]
    v, src, first, second, *matrix = call(
        first_kernel,
        [
            region, region, side, side, (rows * cols * slots + cols * cols, size),
            (rows * cols, size, size), (rows * cols * slots, size, size), (cols, size, size),
        ],
        [HBM] * 12,
        [
            pltpu.with_memory_space_constraint(x, pltpu.HBM)
            for x in small
            + [
                self_tiles.reshape(rows * cols, size, size),
                edge_tiles.reshape(rows * cols * slots, size, size),
            ]
        ],
        staged
        + [field]
        + [pltpu.SemaphoreType.DMA((n,)) for n in (len(small), rows, rows)],
        limit=10,
    )
    total, src, rim1, rim2 = exchange(v, first, second, src)

    operands = matrix + [total, src, rim1, rim2]
    v, s, jac, first, second = call(
        second_kernel, [region] * 3 + [side] * 2, [VMEM] * len(operands), operands, [field]
    )
    total, rim1, rim2 = exchange(v, first, second)

    operands = matrix + [total, src, s, jac, rim1, rim2]
    v, w, first, second, sums = call(
        third_kernel,
        [region] * 2 + [side] * 2 + [(peers, size)],
        [VMEM] * len(operands), operands, [field],
    )
    gathered = lax.all_to_all(sums, ("slab", "cross"), 0, 0, tiled=True)
    total, rim1, rim2 = exchange(v, first, second)

    return tuple(
        pl.pallas_call(
            functools.partial(last_kernel, rows, cols),
            out_shape=[jax.ShapeDtypeStruct((rows, cols, size), f32)] * 2,
            in_specs=[VMEM] * 7,
            out_specs=[VMEM] * 2,
            scratch_shapes=[pltpu.VMEM(region, f32)],
            compiler_params=pltpu.CompilerParams(vmem_limit_bytes=2 << 20),
        )(gathered, total, rim1, rim2, s, jac, w)
    )


def solution(mesh):
    in_specs = (
        P(None, "slab", "cross", None),
        P(None, "slab", "cross", None),
        P(None, "slab", "cross", None),
        P("slab", "cross", None),
        P("slab", "cross", None),
        P("slab", "cross", None, None),
        P("slab", "cross", None, None, None),
        P("slab", "cross"),
        P("slab", "cross", None),
        P("cross"),
        P("cross", None),
        P("cross", None),
    )
    out_specs = (P("slab", "cross", None), P("slab", "cross", None))
    return jax.shard_map(
        per_device, mesh=mesh, in_specs=in_specs, out_specs=out_specs, check_vma=False
    )
```

```python
import functools

import jax
import jax.numpy as jnp
from jax import lax
from jax.experimental import pallas as pl
from jax.experimental.pallas import tpu as pltpu
from jax.sharding import PartitionSpec as P


STRIDE = 8
CODE_STEP = (1, STRIDE - 1, STRIDE, STRIDE + 1)

VMEM = pl.BlockSpec(memory_space=pltpu.VMEM)
HBM = pl.BlockSpec(memory_space=pltpu.HBM)
f32 = jnp.float32


def inside_grid(rows, cols, shape):
    slab, cross = lax.axis_index("slab"), lax.axis_index("cross")
    has_south = slab < lax.axis_size("slab") - 1
    at = lax.broadcasted_iota(jnp.int32, shape, 0)
    column = at % STRIDE
    first = jnp.where(cross > 0, 0, 1)
    last = jnp.where(cross < lax.axis_size("cross") - 1, cols + 1, cols)
    end = jnp.where(has_south, rows + 1, rows) * STRIDE
    own = (at < rows * STRIDE) & (column >= 1) & (column <= cols)
    return (column >= first) & (column <= last) & (at < end), own


class Tiles:
    def __init__(self, rows, cols, p_ref, mask, selfs, edges, ghosts):
        self.rows, self.cols, self.p_ref, self.mask = rows, cols, p_ref, mask
        self.selfs, self.edges, self.ghosts = selfs, edges, ghosts
        self.size = p_ref.shape[1]
        full = (self.size, self.size)
        self.lane = lax.broadcasted_iota(jnp.int32, full, 1)
        self.columns = jnp.transpose(p_ref[...])
        self.sums = jnp.zeros(full, f32)
        self.parts = {}

    def fold(self, product, at, factor=None):
        part = jnp.sum(product.reshape(self.size // 8, 8, self.size), axis=0)
        if factor is not None:
            part = part * factor
        self.parts[at] = self.parts[at] + part if at in self.parts else part

    def block(self, r, c):
        size, cols = self.size, self.cols
        at = r * STRIDE + c + 1
        down = jnp.broadcast_to(self.columns[:, at : at + 1], (size, size))
        tile = self.selfs[r * cols + c]
        acc = tile * self.p_ref[at : at + 1, :]
        self.fold(tile * down, at)
        for code, distance in enumerate(CODE_STEP):
            slot = (r * cols + c) * len(CODE_STEP) + code
            live = self.mask[slot : slot + 1, :]
            j = at + distance
            tile = self.edges[slot]
            acc += tile * (self.p_ref[j : j + 1, :] * live)
            self.fold(tile * down, j, live)
        if r == self.rows - 1:
            tile = self.ghosts[c]
            base = self.rows * cols * len(CODE_STEP) + c * cols
            field = jnp.zeros((1, size), f32)
            for o in range(cols):
                j = r * STRIDE + 1 + o
                field += self.p_ref[j : j + 1, :] * self.mask[base + o : base + o + 1, :]
            acc += tile * field
            part = jnp.sum((tile * down).reshape(size // 8, 8, size), axis=0)
            for o in range(cols):
                j = r * STRIDE + 1 + o
                self.parts[j] += part * self.mask[base + o : base + o + 1, :]
        self.sums = jnp.where(self.lane == at, jnp.sum(acc, axis=1, keepdims=True), self.sums)

    def store(self, v_ref):
        v_ref[...] += jnp.transpose(self.sums)[: v_ref.shape[0], :]
        for at, part in self.parts.items():
            v_ref[at : at + 1, :] += jnp.sum(part, axis=0, keepdims=True)


def on_even(axis):
    return lax.axis_index(axis) % 2 == 0


def pack_sides(v_ref, first, second, rows, cols):
    even = on_even("cross")
    for r in range(rows + 1):
        east = v_ref[r * STRIDE + cols : r * STRIDE + cols + 2, :]
        west = v_ref[r * STRIDE : r * STRIDE + 2, :]
        first[2 * r : 2 * r + 2, :] = jnp.where(even, east, west)
        second[2 * r : 2 * r + 2, :] = jnp.where(even, west, east)


def first_kernel(rows, cols, *refs):
    inputs, refs = refs[:12], refs[12:]
    (v_out, src_out, first, second, mask, selfs, edges, ghosts), refs = refs[:8], refs[8:]
    staged, (self_in, edge_in, small_sem, self_sem, edge_sem) = refs[:10], refs[10:]
    self_hbm, edge_hbm = inputs[10:]
    size = v_out.shape[1]
    slots = len(CODE_STEP)
    small = [
        pltpu.make_async_copy(hbm, here, small_sem.at[k])
        for k, (hbm, here) in enumerate(zip(inputs[:10], staged))
    ]
    for copy in small:
        copy.start()
    for r in range(rows):
        part = pl.ds(r * cols, cols)
        pltpu.make_async_copy(self_hbm.at[part], self_in.at[part], self_sem.at[r]).start()
    for r in range(rows):
        part = pl.ds(r * cols * slots, cols * slots)
        pltpu.make_async_copy(edge_hbm.at[part], edge_in.at[part], edge_sem.at[r]).start()
    count, offset, owner, mirror, gain, vel, acc, grad, dens, weight = staged
    for copy in small:
        copy.wait()
    base = rows * cols * slots
    for c in range(cols):
        for o in range(cols):
            same = jnp.where(owner[c] == o, 1.0, 0.0)
            mask[base + c * cols + o : base + c * cols + o + 1, :] = jnp.full((1, size), same, f32)

    v_out[...] = jnp.zeros_like(v_out)
    src_out[...] = jnp.zeros_like(src_out)
    even = on_even("cross")
    for r in range(rows):
        lo = r * STRIDE + 1
        total = jnp.zeros((cols, size), f32)
        for d in range(3):
            total += grad[d, r] * (vel[d, r] + 0.5 * acc[d, r])
        src = dens[r] / 0.25 - total / 0.5
        src_out[lo : lo + cols, :] = src
        v_out[lo : lo + cols, :] = -weight[r]
        head = 2 * (rows + 1) + r
        east, west = src[cols - 1 : cols, :], src[0:1, :]
        first[head : head + 1, :] = jnp.where(even, east, west)
        second[head : head + 1, :] = jnp.where(even, west, east)
    for side in (first, second):
        for row in range(2 * (rows + 1) + rows, side.shape[0]):
            side[row : row + 1, :] = jnp.zeros((1, size), f32)

    on_wall = lax.axis_index("slab") == lax.axis_size("slab") - 1
    pad = jnp.zeros((size - cols, size), f32)
    mirrors = jnp.transpose(jnp.concatenate([mirror[...].astype(f32), pad], axis=0))
    gains = jnp.transpose(
        jnp.concatenate([gain[...] * jnp.where(on_wall, -1.0, 0.0), pad], axis=0)
    )
    lane = lax.broadcasted_iota(jnp.int32, (size, size), 1)
    eye = lane == lax.broadcasted_iota(jnp.int32, (size, size), 0)
    lanef = lane.astype(f32)
    for c in range(cols):
        hit = lanef == mirrors[:, c : c + 1]
        tile = jnp.where(hit, gains[:, c : c + 1], 0.0)
        other = jnp.where(owner[c] == c, 0.0, 1.0)
        ghosts[c] = jnp.where(eye, tile * other, tile)

    has_south = lax.axis_index("slab") < lax.axis_size("slab") - 1
    has_west = lax.axis_index("cross") > 0
    has_east = lax.axis_index("cross") < lax.axis_size("cross") - 1
    sums = jnp.zeros((size, size), f32)
    for r in range(rows):
        part = pl.ds(r * cols, cols)
        pltpu.make_async_copy(self_hbm.at[part], self_in.at[part], self_sem.at[r]).wait()
        part = pl.ds(r * cols * slots, cols * slots)
        pltpu.make_async_copy(edge_hbm.at[part], edge_in.at[part], edge_sem.at[r]).wait()
        for c in range(cols):
            block = r * cols + c
            at = r * STRIDE + c + 1
            tile = jnp.where(eye, 0.0, self_in[block])
            selfs[block] = tile
            rowwise = tile
            v_out[at : at + 1, :] += jnp.sum(tile, axis=0, keepdims=True)
            for k in range(slots):
                code = offset[r, c, k]
                place = block * slots + code
                live = jnp.where(k < count[r, c], 1.0, 0.0)
                mask[pl.ds(place, 1), :] = jnp.full((1, size), live, f32)
                there = jnp.asarray(True)
                if c == 0:
                    there = there & (has_west | (code != 1))
                if c == cols - 1:
                    there = there & (has_east | ((code != 0) & (code != 3)))
                if r == rows - 1:
                    there = there & (has_south | (code == 0))
                tile = edge_in[block * slots + k]
                edges[place] = tile
                rowwise += tile * jnp.where(there, live, 0.0)
                step = jnp.where(code == 0, CODE_STEP[0], CODE_STEP[1] - 1 + code)
                v_out[pl.ds(at + step, 1), :] += jnp.sum(tile, axis=0, keepdims=True) * live
            if r == rows - 1:
                tile = ghosts[c]
                rowwise += tile
                j = r * STRIDE + 1 + owner[c]
                v_out[pl.ds(j, 1), :] += jnp.sum(tile, axis=0, keepdims=True)
            sums = jnp.where(lane == at, jnp.sum(rowwise, axis=1, keepdims=True), sums)
    v_out[...] += jnp.transpose(sums)[: v_out.shape[0], :]
    pack_sides(v_out, first, second, rows, cols)


def add_rims(rows, total, first, second, out):
    even = on_even("slab")
    has_north = lax.axis_index("slab") > 0
    out[...] = total[...]
    north = jnp.where(even, second[:STRIDE, :], first[:STRIDE, :])
    out[:STRIDE, :] += jnp.where(has_north, north, 0.0)
    out[rows * STRIDE :, :] += jnp.where(even, first[:STRIDE, :], second[:STRIDE, :])


def second_kernel(
    rows, cols, mask, selfs, edges, ghosts, total, src, rim1, rim2,
    v_out, s_out, jac_out, side1, side2, p_ref,
):
    inside, _ = inside_grid(rows, cols, v_out.shape)
    add_rims(rows, total, rim1, rim2, jac_out)
    s_out[...] = src[...]
    s_out[rows * STRIDE :, :] = jnp.where(
        on_even("slab"), rim1[STRIDE:, :], rim2[STRIDE:, :]
    )
    jac = jnp.where(inside, -jac_out[...], 1.0)
    s = jnp.where(inside, s_out[...] / jac, 0.0)
    p_ref[...] = jnp.zeros_like(p_ref)
    p_ref[: s.shape[0], :] = s
    s_out[...] = s
    jac_out[...] = jac
    v_out[...] = jnp.zeros_like(v_out)
    tiles = Tiles(rows, cols, p_ref, mask, selfs, edges, ghosts)
    for r in range(rows):
        for c in range(cols):
            tiles.block(r, c)
    tiles.store(v_out)
    for side in (side1, side2):
        side[...] = jnp.zeros_like(side)
    pack_sides(v_out, side1, side2, rows, cols)


def third_kernel(
    rows, cols, mask, selfs, edges, ghosts, total, src, s_ref, jac, rim1, rim2,
    v_out, w_out, side1, side2, sums_out, p_ref,
):
    size = p_ref.shape[1]
    inside, own = inside_grid(rows, cols, v_out.shape)
    add_rims(rows, total, rim1, rim2, w_out)
    u = w_out[...]
    w = jnp.where(inside, u / jac[...], 0.0)
    p_ref[...] = jnp.zeros_like(p_ref)
    p_ref[: w.shape[0], :] = w
    w_out[...] = w
    v_out[...] = jnp.zeros_like(v_out)
    tiles = Tiles(rows, cols, p_ref, mask, selfs, edges, ghosts)
    for r in range(rows):
        for c in range(cols):
            tiles.block(r, c)
    tiles.store(v_out)
    for side in (side1, side2):
        side[...] = jnp.zeros_like(side)
    pack_sides(v_out, side1, side2, rows, cols)
    s = s_ref[...]

    def whole(x):
        return jnp.sum(jnp.sum(x, axis=0, keepdims=True), axis=1, keepdims=True)

    sums = (
        whole(jnp.where(own, src[...] * s, 0.0)),
        whole(jnp.where(own, s * u, 0.0)),
        whole(jnp.where(own, w * u, 0.0)),
        whole(w * v_out[...]),
    )
    lane = lax.broadcasted_iota(jnp.int32, (1, size), 1)
    line = jnp.zeros((1, size), f32)
    for k, value in enumerate(sums):
        line = jnp.where(lane == k, value, line)
    sums_out[...] = jnp.broadcast_to(line, sums_out.shape)


def merge_kernel(rows, cols, with_src, *refs):
    v, side1, side2 = refs[:3]
    total, first, second = refs[3 + with_src : 6 + with_src]
    even = on_even("cross")
    has_west = lax.axis_index("cross") > 0
    has_east = lax.axis_index("cross") < lax.axis_size("cross") - 1
    west = jnp.where(even, side2[...], side1[...])
    east = jnp.where(even, side1[...], side2[...])
    west = jnp.where(has_west, west, 0.0)
    east = jnp.where(has_east, east, 0.0)
    total[...] = v[...]
    for r in range(rows + 1):
        lo = r * STRIDE
        total[lo : lo + 2, :] += west[2 * r : 2 * r + 2, :]
        total[lo + cols : lo + cols + 2, :] += east[2 * r : 2 * r + 2, :]
    top, bottom = total[:STRIDE, :], total[rows * STRIDE :, :]
    even = on_even("slab")
    first[:STRIDE, :] = jnp.where(even, bottom, top)
    second[:STRIDE, :] = jnp.where(even, top, bottom)
    if with_src:
        src, src_out = refs[3], refs[7]
        src_out[...] = src[...]
        for r in range(rows):
            lo, head = r * STRIDE, 2 * (rows + 1) + r
            src_out[lo : lo + 1, :] = west[head : head + 1, :]
            src_out[lo + cols + 1 : lo + cols + 2, :] = east[head : head + 1, :]
        for out in (first, second):
            out[STRIDE:, :] = src_out[:STRIDE, :]


def last_kernel(
    rows, cols, gathered, total, rim1, rim2, s_ref, jac_ref, w_ref, pressure, residual, v
):
    add_rims(rows, total, rim1, rim2, v)
    nu = jnp.sum(gathered[...], axis=0, keepdims=True)
    nu0, nu1, nu2, nu3 = (nu[:, k : k + 1] for k in range(4))
    rho = nu1 / nu0
    a0 = 1.0 / (1.0 + rho)
    norm1 = a0 * a0 * (nu2 - rho * nu1)
    beta = norm1 / nu0
    g = a0 * rho + beta
    cross = g * g * nu1 - 2.0 * g * a0 * nu2 + a0 * a0 * nu3
    sigma = jnp.where(norm1 > 0.0, beta + cross / norm1, 0.0)
    step = 1.0 / (1.0 + sigma)
    rest = sigma * step
    ps, pw = a0 + step * g, -step * a0
    rs, rw, rv = a0 * rho * rest - step * beta, -a0 * rest - step * g, step * a0
    for r in range(rows):
        lo = r * STRIDE + 1
        s, w, jac = s_ref[lo : lo + cols, :], w_ref[lo : lo + cols, :], jac_ref[lo : lo + cols, :]
        pressure[r] = ps * s + pw * w
        residual[r] = jac * (rs * s + rw * w) + rv * v[lo : lo + cols, :]


def swap(value, second, axis):
    slabs, crosses = lax.axis_size("slab"), lax.axis_size("cross")
    pairs = []
    for a in range(slabs):
        for c in range(crosses):
            if axis == "cross":
                to = (a, (((c + 1) ^ 1) - 1) % crosses if second else c ^ 1)
            elif not second:
                to = (a ^ 1, c)
            elif 0 < a < slabs - 1:
                to = (((a + 1) ^ 1) - 1, c)
            else:
                to = (a, c ^ 1)
            pairs.append((a * crosses + c, to[0] * crosses + to[1]))
    return lax.ppermute(value, ("slab", "cross"), pairs)


def per_device(
    velocity,
    acceleration,
    grad_coef,
    density_dev,
    self_weight,
    self_tiles,
    edge_tiles,
    tile_count,
    tile_offset,
    ghost_owner,
    ghost_mirror,
    ghost_gain,
):
    rows, cols, size = self_weight.shape
    slots = tile_offset.shape[-1]
    region = ((rows + 1) * STRIDE, size)
    side = (STRIDE * pl.cdiv(2 * (rows + 1) + rows, STRIDE), size)
    line = (STRIDE, size)
    peers = lax.axis_size("slab") * lax.axis_size("cross")

    def call(kernel, shapes, specs, operands, scratch=(), extra=(), limit=2):
        return pl.pallas_call(
            functools.partial(kernel, rows, cols, *extra),
            out_shape=[pltpu.VMEM(shape, f32) for shape in shapes],
            in_specs=specs,
            out_specs=[VMEM] * len(shapes),
            scratch_shapes=list(scratch),
            compiler_params=pltpu.CompilerParams(vmem_limit_bytes=limit << 20),
        )(*operands)

    def exchange(v, first, second, src=None):
        first = swap(first, False, "cross")
        second = swap(second, True, "cross")
        operands = [v, first, second]
        shapes = [region, line, line]
        if src is not None:
            operands.append(src)
            shapes = [region, (2 * STRIDE, size), (2 * STRIDE, size), region]
        total, first, second, *rest = call(
            merge_kernel, shapes, [VMEM] * len(operands), operands, extra=(src is not None,)
        )
        return [total, *rest, swap(first, False, "slab"), swap(second, True, "slab")]

    field = pltpu.VMEM((size, size), f32)
    small = [
        tile_count, tile_offset, ghost_owner, ghost_mirror, ghost_gain,
        velocity, acceleration, grad_coef, density_dev, self_weight,
    ]
    staged = [
        (pltpu.SMEM if k < 3 else pltpu.VMEM)(x.shape, x.dtype) for k, x in enumerate(small)
    ]
    v, src, first, second, *matrix = call(
        first_kernel,
        [
            region, region, side, side, (rows * cols * slots + cols * cols, size),
            (rows * cols, size, size), (rows * cols * slots, size, size), (cols, size, size),
        ],
        [HBM] * 12,
        [
            pltpu.with_memory_space_constraint(x, pltpu.HBM)
            for x in small
            + [
                self_tiles.reshape(rows * cols, size, size),
                edge_tiles.reshape(rows * cols * slots, size, size),
            ]
        ],
        staged
        + [pltpu.VMEM((n, size, size), f32) for n in (rows * cols, rows * cols * slots)]
        + [pltpu.SemaphoreType.DMA((n,)) for n in (len(small), rows, rows)],
        limit=16,
    )
    total, src, rim1, rim2 = exchange(v, first, second, src)

    operands = matrix + [total, src, rim1, rim2]
    v, s, jac, first, second = call(
        second_kernel, [region] * 3 + [side] * 2, [VMEM] * len(operands), operands, [field]
    )
    total, rim1, rim2 = exchange(v, first, second)

    operands = matrix + [total, src, s, jac, rim1, rim2]
    v, w, first, second, sums = call(
        third_kernel,
        [region] * 2 + [side] * 2 + [(peers, size)],
        [VMEM] * len(operands), operands, [field],
    )
    gathered = lax.all_to_all(sums, ("slab", "cross"), 0, 0, tiled=True)
    total, rim1, rim2 = exchange(v, first, second)

    return tuple(
        pl.pallas_call(
            functools.partial(last_kernel, rows, cols),
            out_shape=[jax.ShapeDtypeStruct((rows, cols, size), f32)] * 2,
            in_specs=[VMEM] * 7,
            out_specs=[VMEM] * 2,
            scratch_shapes=[pltpu.VMEM(region, f32)],
            compiler_params=pltpu.CompilerParams(vmem_limit_bytes=2 << 20),
        )(gathered, total, rim1, rim2, s, jac, w)
    )


def solution(mesh):
    in_specs = (
        P(None, "slab", "cross", None),
        P(None, "slab", "cross", None),
        P(None, "slab", "cross", None),
        P("slab", "cross", None),
        P("slab", "cross", None),
        P("slab", "cross", None, None),
        P("slab", "cross", None, None, None),
        P("slab", "cross"),
        P("slab", "cross", None),
        P("cross"),
        P("cross", None),
        P("cross", None),
    )
    out_specs = (P("slab", "cross", None), P("slab", "cross", None))
    return jax.shard_map(
        per_device, mesh=mesh, in_specs=in_specs, out_specs=out_specs, check_vma=False
    )
```

```python
import functools

import jax
import jax.numpy as jnp
from jax import lax
from jax.experimental import pallas as pl
from jax.experimental.pallas import tpu as pltpu
from jax.sharding import PartitionSpec as P


STRIDE = 8
CODE_STEP = (1, STRIDE - 1, STRIDE, STRIDE + 1)

VMEM = pl.BlockSpec(memory_space=pltpu.VMEM)
HBM = pl.BlockSpec(memory_space=pltpu.HBM)
f32 = jnp.float32


def inside_grid(rows, cols, shape):
    slab, cross = lax.axis_index("slab"), lax.axis_index("cross")
    has_south = slab < lax.axis_size("slab") - 1
    at = lax.broadcasted_iota(jnp.int32, shape, 0)
    column = at % STRIDE
    first = jnp.where(cross > 0, 0, 1)
    last = jnp.where(cross < lax.axis_size("cross") - 1, cols + 1, cols)
    end = jnp.where(has_south, rows + 1, rows) * STRIDE
    own = (at < rows * STRIDE) & (column >= 1) & (column <= cols)
    return (column >= first) & (column <= last) & (at < end), own


class Tiles:
    def __init__(self, rows, cols, p_ref, mask, selfs, edges, ghosts):
        self.rows, self.cols, self.p_ref, self.mask = rows, cols, p_ref, mask
        self.selfs, self.edges, self.ghosts = selfs, edges, ghosts
        self.size = p_ref.shape[1]
        full = (self.size, self.size)
        self.lane = lax.broadcasted_iota(jnp.int32, full, 1)
        self.eye = self.lane == lax.broadcasted_iota(jnp.int32, full, 0)
        self.columns = jnp.transpose(p_ref[...])
        self.sums = jnp.zeros(full, f32)
        self.parts = {}

    def fold(self, product, at, factor=None):
        part = jnp.sum(product.reshape(self.size // 8, 8, self.size), axis=0)
        if factor is not None:
            part = part * factor
        self.parts[at] = self.parts[at] + part if at in self.parts else part

    def block(self, r, c, codes=(0, 1, 2, 3), local=True):
        size, cols = self.size, self.cols
        at = r * STRIDE + c + 1
        down = jnp.broadcast_to(self.columns[:, at : at + 1], (size, size))
        acc = None
        if local:
            tile = jnp.where(self.eye, 0.0, self.selfs[r * cols + c])
            acc = tile * self.p_ref[at : at + 1, :]
            self.fold(tile * down, at)
        for code in codes:
            slot = (r * cols + c) * len(CODE_STEP) + code
            live = self.mask[slot : slot + 1, :]
            j = at + CODE_STEP[code]
            tile = self.edges[slot]
            product = tile * (self.p_ref[j : j + 1, :] * live)
            acc = product if acc is None else acc + product
            self.fold(tile * down, j, live)
        if local and r == self.rows - 1:
            tile = self.ghosts[c]
            base = self.rows * cols * len(CODE_STEP) + c * cols
            field = jnp.zeros((1, size), f32)
            for o in range(cols):
                j = r * STRIDE + 1 + o
                field += self.p_ref[j : j + 1, :] * self.mask[base + o : base + o + 1, :]
            acc += tile * field
            product = tile * down
            for o in range(cols):
                self.fold(product, r * STRIDE + 1 + o, self.mask[base + o : base + o + 1, :])
        self.sums = jnp.where(self.lane == at, jnp.sum(acc, axis=1, keepdims=True), self.sums)

    def early(self):
        for r in range(1, self.rows):
            for c in range(self.cols):
                self.block(r, c, (0, 1, 2, 3) if r < self.rows - 1 else (0,))

    def late(self):
        for c in range(self.cols):
            self.block(0, c)
        for c in range(self.cols):
            self.block(self.rows - 1, c, (1, 2, 3), False)

    def store(self, v_ref):
        v_ref[...] += jnp.transpose(self.sums)[: v_ref.shape[0], :]
        for at, part in self.parts.items():
            v_ref[at : at + 1, :] += jnp.sum(part, axis=0, keepdims=True)


def on_even(axis):
    return lax.axis_index(axis) % 2 == 0


def pack_sides(v_ref, first, second, rows, cols):
    even = on_even("cross")
    for r in range(rows + 1):
        east = v_ref[r * STRIDE + cols : r * STRIDE + cols + 2, :]
        west = v_ref[r * STRIDE : r * STRIDE + 2, :]
        first[2 * r : 2 * r + 2, :] = jnp.where(even, east, west)
        second[2 * r : 2 * r + 2, :] = jnp.where(even, west, east)


def first_kernel(rows, cols, *refs):
    inputs, refs = refs[:12], refs[12:]
    (v_out, src_out, first, second, mask, selfs, edges, ghosts), refs = refs[:8], refs[8:]
    staged, (p_ref, small_sem, self_sem, edge_sem) = refs[:10], refs[10:]
    self_hbm, edge_hbm = inputs[10:]
    size = p_ref.shape[1]
    slots = len(CODE_STEP)
    small = [
        pltpu.make_async_copy(hbm, here, small_sem.at[k])
        for k, (hbm, here) in enumerate(zip(inputs[:10], staged))
    ]
    for copy in small:
        copy.start()
    for r in range(rows):
        part = pl.ds(r * cols, cols)
        pltpu.make_async_copy(self_hbm.at[part], selfs.at[part], self_sem.at[r]).start()
    count, offset, owner, mirror, gain, vel, acc, grad, dens, weight = staged
    for copy in small[:3]:
        copy.wait()
    for r in range(rows):
        for c in range(cols):
            for k in range(slots):
                slot = (r * cols + c) * slots + k
                place = (r * cols + c) * slots + offset[r, c, k]
                pltpu.make_async_copy(
                    edge_hbm.at[slot], edges.at[place], edge_sem.at[r]
                ).start()
    for r in range(rows):
        for c in range(cols):
            for k in range(slots):
                place = (r * cols + c) * slots + offset[r, c, k]
                live = jnp.where(k < count[r, c], 1.0, 0.0)
                mask[pl.ds(place, 1), :] = jnp.full((1, size), live, f32)
    base = rows * cols * slots
    for c in range(cols):
        for o in range(cols):
            same = jnp.where(owner[c] == o, 1.0, 0.0)
            mask[base + c * cols + o : base + c * cols + o + 1, :] = jnp.full((1, size), same, f32)
    for copy in small[3:]:
        copy.wait()

    inside, _ = inside_grid(rows, cols, v_out.shape)
    p_ref[...] = jnp.zeros_like(p_ref)
    p_ref[: v_out.shape[0], :] = jnp.where(inside, 1.0, 0.0)
    v_out[...] = jnp.zeros_like(v_out)
    src_out[...] = jnp.zeros_like(src_out)
    even = on_even("cross")
    for r in range(rows):
        lo = r * STRIDE + 1
        total = jnp.zeros((cols, size), f32)
        for d in range(3):
            total += grad[d, r] * (vel[d, r] + 0.5 * acc[d, r])
        src = dens[r] / 0.25 - total / 0.5
        src_out[lo : lo + cols, :] = src
        v_out[lo : lo + cols, :] = -weight[r]
        head = 2 * (rows + 1) + r
        east, west = src[cols - 1 : cols, :], src[0:1, :]
        first[head : head + 1, :] = jnp.where(even, east, west)
        second[head : head + 1, :] = jnp.where(even, west, east)
    for side in (first, second):
        for row in range(2 * (rows + 1) + rows, side.shape[0]):
            side[row : row + 1, :] = jnp.zeros((1, size), f32)

    on_wall = lax.axis_index("slab") == lax.axis_size("slab") - 1
    pad = jnp.zeros((size - cols, size), f32)
    mirrors = jnp.transpose(jnp.concatenate([mirror[...].astype(f32), pad], axis=0))
    gains = jnp.transpose(
        jnp.concatenate([gain[...] * jnp.where(on_wall, -1.0, 0.0), pad], axis=0)
    )
    lane = lax.broadcasted_iota(jnp.int32, (size, size), 1)
    sub = lax.broadcasted_iota(jnp.int32, (size, size), 0)
    lanef = lane.astype(f32)
    for c in range(cols):
        hit = lanef == mirrors[:, c : c + 1]
        tile = jnp.where(hit, gains[:, c : c + 1], 0.0)
        other = jnp.where(owner[c] == c, 0.0, 1.0)
        ghosts[c] = jnp.where(lane == sub, tile * other, tile)

    tiles = Tiles(rows, cols, p_ref, mask, selfs, edges, ghosts)
    for r in range(rows):
        part = pl.ds(r * cols, cols)
        pltpu.make_async_copy(self_hbm.at[part], selfs.at[part], self_sem.at[r]).wait()
        part = pl.ds(r * cols * slots, cols * slots)
        pltpu.make_async_copy(edge_hbm.at[part], edges.at[part], edge_sem.at[r]).wait()
        for c in range(cols):
            tiles.block(r, c)
    tiles.store(v_out)
    pack_sides(v_out, first, second, rows, cols)


def add_rims(rows, total, first, second, out):
    even = on_even("slab")
    has_north = lax.axis_index("slab") > 0
    out[...] = total[...]
    north = jnp.where(even, second[:STRIDE, :], first[:STRIDE, :])
    out[:STRIDE, :] += jnp.where(has_north, north, 0.0)
    out[rows * STRIDE :, :] += jnp.where(even, first[:STRIDE, :], second[:STRIDE, :])


def early_kernel(rows, cols, sign, mask, selfs, edges, ghosts, top, bottom, v_out, p_ref):
    inside, _ = inside_grid(rows, cols, v_out.shape)
    at = lax.broadcasted_iota(jnp.int32, v_out.shape, 0)
    known = inside & (at >= STRIDE) & (at < rows * STRIDE)
    field = jnp.where(known, top[...] / jnp.where(known, sign * bottom[...], 1.0), 0.0)
    p_ref[...] = jnp.zeros_like(p_ref)
    p_ref[: field.shape[0], :] = field
    v_out[...] = jnp.zeros_like(v_out)
    tiles = Tiles(rows, cols, p_ref, mask, selfs, edges, ghosts)
    tiles.early()
    tiles.store(v_out)


def second_kernel(
    rows, cols, mask, selfs, edges, ghosts, early, total, src, rim1, rim2,
    v_out, s_out, jac_out, side1, side2, p_ref,
):
    inside, _ = inside_grid(rows, cols, v_out.shape)
    add_rims(rows, total, rim1, rim2, jac_out)
    s_out[...] = src[...]
    s_out[rows * STRIDE :, :] = jnp.where(
        on_even("slab"), rim1[STRIDE:, :], rim2[STRIDE:, :]
    )
    jac = jnp.where(inside, -jac_out[...], 1.0)
    s = jnp.where(inside, s_out[...] / jac, 0.0)
    p_ref[...] = jnp.zeros_like(p_ref)
    p_ref[: s.shape[0], :] = s
    s_out[...] = s
    jac_out[...] = jac
    v_out[...] = early[...]
    tiles = Tiles(rows, cols, p_ref, mask, selfs, edges, ghosts)
    tiles.late()
    tiles.store(v_out)
    for side in (side1, side2):
        side[...] = jnp.zeros_like(side)
    pack_sides(v_out, side1, side2, rows, cols)


def third_kernel(
    rows, cols, mask, selfs, edges, ghosts, early, total, src, s_ref, jac, rim1, rim2,
    v_out, w_out, side1, side2, sums_out, p_ref,
):
    size = p_ref.shape[1]
    inside, own = inside_grid(rows, cols, v_out.shape)
    add_rims(rows, total, rim1, rim2, w_out)
    u = w_out[...]
    w = jnp.where(inside, u / jac[...], 0.0)
    p_ref[...] = jnp.zeros_like(p_ref)
    p_ref[: w.shape[0], :] = w
    w_out[...] = w
    v_out[...] = early[...]
    tiles = Tiles(rows, cols, p_ref, mask, selfs, edges, ghosts)
    tiles.late()
    tiles.store(v_out)
    for side in (side1, side2):
        side[...] = jnp.zeros_like(side)
    pack_sides(v_out, side1, side2, rows, cols)
    s = s_ref[...]

    def whole(x):
        return jnp.sum(jnp.sum(x, axis=0, keepdims=True), axis=1, keepdims=True)

    sums = (
        whole(jnp.where(own, src[...] * s, 0.0)),
        whole(jnp.where(own, s * u, 0.0)),
        whole(jnp.where(own, w * u, 0.0)),
        whole(w * v_out[...]),
    )
    lane = lax.broadcasted_iota(jnp.int32, (1, size), 1)
    line = jnp.zeros((1, size), f32)
    for k, value in enumerate(sums):
        line = jnp.where(lane == k, value, line)
    sums_out[...] = jnp.broadcast_to(line, sums_out.shape)


def merge_kernel(rows, cols, with_src, *refs):
    v, side1, side2 = refs[:3]
    total, first, second = refs[3 + with_src : 6 + with_src]
    even = on_even("cross")
    has_west = lax.axis_index("cross") > 0
    has_east = lax.axis_index("cross") < lax.axis_size("cross") - 1
    west = jnp.where(even, side2[...], side1[...])
    east = jnp.where(even, side1[...], side2[...])
    west = jnp.where(has_west, west, 0.0)
    east = jnp.where(has_east, east, 0.0)
    total[...] = v[...]
    for r in range(rows + 1):
        lo = r * STRIDE
        total[lo : lo + 2, :] += west[2 * r : 2 * r + 2, :]
        total[lo + cols : lo + cols + 2, :] += east[2 * r : 2 * r + 2, :]
    top, bottom = total[:STRIDE, :], total[rows * STRIDE :, :]
    even = on_even("slab")
    first[:STRIDE, :] = jnp.where(even, bottom, top)
    second[:STRIDE, :] = jnp.where(even, top, bottom)
    if with_src:
        src, src_out = refs[3], refs[7]
        src_out[...] = src[...]
        for r in range(rows):
            lo, head = r * STRIDE, 2 * (rows + 1) + r
            src_out[lo : lo + 1, :] = west[head : head + 1, :]
            src_out[lo + cols + 1 : lo + cols + 2, :] = east[head : head + 1, :]
        for out in (first, second):
            out[STRIDE:, :] = src_out[:STRIDE, :]


def last_kernel(
    rows, cols, gathered, total, rim1, rim2, s_ref, jac_ref, w_ref, pressure, residual, v
):
    add_rims(rows, total, rim1, rim2, v)
    nu = jnp.sum(gathered[...], axis=0, keepdims=True)
    nu0, nu1, nu2, nu3 = (nu[:, k : k + 1] for k in range(4))
    rho = nu1 / nu0
    a0 = 1.0 / (1.0 + rho)
    norm1 = a0 * a0 * (nu2 - rho * nu1)
    beta = norm1 / nu0
    g = a0 * rho + beta
    cross = g * g * nu1 - 2.0 * g * a0 * nu2 + a0 * a0 * nu3
    sigma = jnp.where(norm1 > 0.0, beta + cross / norm1, 0.0)
    step = 1.0 / (1.0 + sigma)
    rest = sigma * step
    ps, pw = a0 + step * g, -step * a0
    rs, rw, rv = a0 * rho * rest - step * beta, -a0 * rest - step * g, step * a0
    for r in range(rows):
        lo = r * STRIDE + 1
        s, w, jac = s_ref[lo : lo + cols, :], w_ref[lo : lo + cols, :], jac_ref[lo : lo + cols, :]
        pressure[r] = ps * s + pw * w
        residual[r] = jac * (rs * s + rw * w) + rv * v[lo : lo + cols, :]


def swap(value, second, axis):
    slabs, crosses = lax.axis_size("slab"), lax.axis_size("cross")
    pairs = []
    for a in range(slabs):
        for c in range(crosses):
            if axis == "cross":
                to = (a, (((c + 1) ^ 1) - 1) % crosses if second else c ^ 1)
            elif not second:
                to = (a ^ 1, c)
            elif 0 < a < slabs - 1:
                to = (((a + 1) ^ 1) - 1, c)
            else:
                to = (a, c ^ 1)
            pairs.append((a * crosses + c, to[0] * crosses + to[1]))
    return lax.ppermute(value, ("slab", "cross"), pairs)


def per_device(
    velocity,
    acceleration,
    grad_coef,
    density_dev,
    self_weight,
    self_tiles,
    edge_tiles,
    tile_count,
    tile_offset,
    ghost_owner,
    ghost_mirror,
    ghost_gain,
):
    rows, cols, size = self_weight.shape
    slots = tile_offset.shape[-1]
    region = ((rows + 1) * STRIDE, size)
    side = (STRIDE * pl.cdiv(2 * (rows + 1) + rows, STRIDE), size)
    line = (STRIDE, size)
    peers = lax.axis_size("slab") * lax.axis_size("cross")

    def call(kernel, shapes, specs, operands, scratch=(), extra=(), limit=2):
        return pl.pallas_call(
            functools.partial(kernel, rows, cols, *extra),
            out_shape=[pltpu.VMEM(shape, f32) for shape in shapes],
            in_specs=specs,
            out_specs=[VMEM] * len(shapes),
            scratch_shapes=list(scratch),
            compiler_params=pltpu.CompilerParams(vmem_limit_bytes=limit << 20),
        )(*operands)

    def exchange(v, first, second, src=None):
        first = swap(first, False, "cross")
        second = swap(second, True, "cross")
        operands = [v, first, second]
        shapes = [region, line, line]
        if src is not None:
            operands.append(src)
            shapes = [region, (2 * STRIDE, size), (2 * STRIDE, size), region]
        total, first, second, *rest = call(
            merge_kernel, shapes, [VMEM] * len(operands), operands, extra=(src is not None,)
        )
        first = swap(first, False, "slab")
        second = swap(second, True, "slab")
        return [total, *rest, first, second]

    def early(top, bottom, sign):
        operands = matrix + [top, bottom]
        return call(early_kernel, [region], [VMEM] * len(operands), operands, [field], (sign,))[0]

    field = pltpu.VMEM((size, size), f32)
    small = [
        tile_count, tile_offset, ghost_owner, ghost_mirror, ghost_gain,
        velocity, acceleration, grad_coef, density_dev, self_weight,
    ]
    staged = [
        (pltpu.SMEM if k < 3 else pltpu.VMEM)(x.shape, x.dtype) for k, x in enumerate(small)
    ]
    v, src, first, second, *matrix = call(
        first_kernel,
        [
            region, region, side, side, (rows * cols * slots + cols * cols, size),
            (rows * cols, size, size), (rows * cols * slots, size, size), (cols, size, size),
        ],
        [HBM] * 12,
        [
            pltpu.with_memory_space_constraint(x, pltpu.HBM)
            for x in small
            + [
                self_tiles.reshape(rows * cols, size, size),
                edge_tiles.reshape(rows * cols * slots, size, size),
            ]
        ],
        staged
        + [field]
        + [pltpu.SemaphoreType.DMA((n,)) for n in (len(small), rows, rows)],
        limit=10,
    )
    total, src, rim1, rim2 = exchange(v, first, second, src)
    part = early(src, total, -1.0)

    operands = matrix + [part, total, src, rim1, rim2]
    v, s, jac, first, second = call(
        second_kernel, [region] * 3 + [side] * 2, [VMEM] * len(operands), operands, [field]
    )
    total, rim1, rim2 = exchange(v, first, second)
    part = early(total, jac, 1.0)

    operands = matrix + [part, total, src, s, jac, rim1, rim2]
    v, w, first, second, sums = call(
        third_kernel,
        [region] * 2 + [side] * 2 + [(peers, size)],
        [VMEM] * len(operands), operands, [field],
    )
    gathered = lax.all_to_all(sums, ("slab", "cross"), 0, 0, tiled=True)
    total, rim1, rim2 = exchange(v, first, second)

    return tuple(
        pl.pallas_call(
            functools.partial(last_kernel, rows, cols),
            out_shape=[jax.ShapeDtypeStruct((rows, cols, size), f32)] * 2,
            in_specs=[VMEM] * 7,
            out_specs=[VMEM] * 2,
            scratch_shapes=[pltpu.VMEM(region, f32)],
            compiler_params=pltpu.CompilerParams(vmem_limit_bytes=2 << 20),
        )(gathered, total, rim1, rim2, s, jac, w)
    )


def solution(mesh):
    in_specs = (
        P(None, "slab", "cross", None),
        P(None, "slab", "cross", None),
        P(None, "slab", "cross", None),
        P("slab", "cross", None),
        P("slab", "cross", None),
        P("slab", "cross", None, None),
        P("slab", "cross", None, None, None),
        P("slab", "cross"),
        P("slab", "cross", None),
        P("cross"),
        P("cross", None),
        P("cross", None),
    )
    out_specs = (P("slab", "cross", None), P("slab", "cross", None))
    return jax.shard_map(
        per_device, mesh=mesh, in_specs=in_specs, out_specs=out_specs, check_vma=False
    )
```

```python
import functools

import jax
import jax.numpy as jnp
from jax import lax
from jax.experimental import pallas as pl
from jax.experimental.pallas import tpu as pltpu
from jax.sharding import PartitionSpec as P


STRIDE = 8
CODE_STEP = (1, STRIDE - 1, STRIDE, STRIDE + 1)

VMEM = pl.BlockSpec(memory_space=pltpu.VMEM)
SMEM = pl.BlockSpec(memory_space=pltpu.SMEM)
HBM = pl.BlockSpec(memory_space=pltpu.HBM)
f32 = jnp.float32


def inside_grid(rows, cols, shape):
    slab, cross = lax.axis_index("slab"), lax.axis_index("cross")
    has_south = slab < lax.axis_size("slab") - 1
    at = lax.broadcasted_iota(jnp.int32, shape, 0)
    column = at % STRIDE
    first = jnp.where(cross > 0, 0, 1)
    last = jnp.where(cross < lax.axis_size("cross") - 1, cols + 1, cols)
    end = jnp.where(has_south, rows + 1, rows) * STRIDE
    own = (at < rows * STRIDE) & (column >= 1) & (column <= cols)
    return (column >= first) & (column <= last) & (at < end), own


class Tiles:
    def __init__(self, rows, cols, p_ref, mask, selfs, edges, ghosts):
        self.rows, self.cols, self.p_ref, self.mask = rows, cols, p_ref, mask
        self.selfs, self.edges, self.ghosts = selfs, edges, ghosts
        self.size = p_ref.shape[1]
        full = (self.size, self.size)
        self.lane = lax.broadcasted_iota(jnp.int32, full, 1)
        self.columns = jnp.transpose(p_ref[...])
        self.sums = jnp.zeros(full, f32)
        self.parts = {}

    def fold(self, product, at, factor=None):
        part = jnp.sum(product.reshape(self.size // 8, 8, self.size), axis=0)
        if factor is not None:
            part = part * factor
        self.parts[at] = self.parts[at] + part if at in self.parts else part

    def block(self, r, c, codes=(0, 1, 2, 3), local=True):
        size, cols = self.size, self.cols
        at = r * STRIDE + c + 1
        down = jnp.broadcast_to(self.columns[:, at : at + 1], (size, size))
        acc = None
        if local:
            tile = self.selfs[r * cols + c]
            acc = tile * self.p_ref[at : at + 1, :]
            self.fold(tile * down, at)
        for code in codes:
            slot = (r * cols + c) * len(CODE_STEP) + code
            live = self.mask[slot : slot + 1, :]
            j = at + CODE_STEP[code]
            tile = self.edges[slot]
            product = tile * (self.p_ref[j : j + 1, :] * live)
            acc = product if acc is None else acc + product
            self.fold(tile * down, j, live)
        if local and r == self.rows - 1:
            tile = self.ghosts[c]
            base = self.rows * cols * len(CODE_STEP) + c * cols
            field = jnp.zeros((1, size), f32)
            for o in range(cols):
                j = r * STRIDE + 1 + o
                field += self.p_ref[j : j + 1, :] * self.mask[base + o : base + o + 1, :]
            acc += tile * field
            product = tile * down
            for o in range(cols):
                self.fold(product, r * STRIDE + 1 + o, self.mask[base + o : base + o + 1, :])
        self.sums = jnp.where(self.lane == at, jnp.sum(acc, axis=1, keepdims=True), self.sums)

    def early(self):
        for r in range(1, self.rows):
            for c in range(self.cols):
                self.block(r, c, (0, 1, 2, 3) if r < self.rows - 1 else (0,))

    def late(self):
        for c in range(self.cols):
            self.block(0, c)
        for c in range(self.cols):
            self.block(self.rows - 1, c, (1, 2, 3), False)

    def store(self, v_ref):
        v_ref[...] += jnp.transpose(self.sums)[: v_ref.shape[0], :]
        for at, part in self.parts.items():
            v_ref[at : at + 1, :] += jnp.sum(part, axis=0, keepdims=True)


def on_even(axis):
    return lax.axis_index(axis) % 2 == 0


def pack_sides(v_ref, first, second, rows, cols):
    even = on_even("cross")
    for r in range(rows + 1):
        east = v_ref[r * STRIDE + cols : r * STRIDE + cols + 2, :]
        west = v_ref[r * STRIDE : r * STRIDE + 2, :]
        first[2 * r : 2 * r + 2, :] = jnp.where(even, east, west)
        second[2 * r : 2 * r + 2, :] = jnp.where(even, west, east)


def first_kernel(rows, cols, *refs):
    inputs, refs = refs[:12], refs[12:]
    (v_out, src_out, first, second, self_in, edge_in, ghosts), refs = refs[:7], refs[7:]
    staged, (small_sem, self_sem, edge_sem) = refs[:10], refs[10:]
    self_hbm, edge_hbm = inputs[10:]
    size = v_out.shape[1]
    slots = len(CODE_STEP)
    small = [
        pltpu.make_async_copy(hbm, here, small_sem.at[k])
        for k, (hbm, here) in enumerate(zip(inputs[:10], staged))
    ]
    for copy in small:
        copy.start()
    for r in range(rows):
        part = pl.ds(r * cols, cols)
        pltpu.make_async_copy(self_hbm.at[part], self_in.at[part], self_sem.at[r]).start()
    for r in range(rows):
        part = pl.ds(r * cols * slots, cols * slots)
        pltpu.make_async_copy(edge_hbm.at[part], edge_in.at[part], edge_sem.at[r]).start()
    count, offset, owner, mirror, gain, vel, acc, grad, dens, weight = staged
    for copy in small:
        copy.wait()
    v_out[...] = jnp.zeros_like(v_out)
    src_out[...] = jnp.zeros_like(src_out)
    even = on_even("cross")
    for r in range(rows):
        lo = r * STRIDE + 1
        total = jnp.zeros((cols, size), f32)
        for d in range(3):
            total += grad[d, r] * (vel[d, r] + 0.5 * acc[d, r])
        src = dens[r] / 0.25 - total / 0.5
        src_out[lo : lo + cols, :] = src
        v_out[lo : lo + cols, :] = -weight[r]
        head = 2 * (rows + 1) + r
        east, west = src[cols - 1 : cols, :], src[0:1, :]
        first[head : head + 1, :] = jnp.where(even, east, west)
        second[head : head + 1, :] = jnp.where(even, west, east)
    for side in (first, second):
        for row in range(2 * (rows + 1) + rows, side.shape[0]):
            side[row : row + 1, :] = jnp.zeros((1, size), f32)

    on_wall = lax.axis_index("slab") == lax.axis_size("slab") - 1
    pad = jnp.zeros((size - cols, size), f32)
    mirrors = jnp.transpose(jnp.concatenate([mirror[...].astype(f32), pad], axis=0))
    gains = jnp.transpose(
        jnp.concatenate([gain[...] * jnp.where(on_wall, -1.0, 0.0), pad], axis=0)
    )
    lane = lax.broadcasted_iota(jnp.int32, (size, size), 1)
    eye = lane == lax.broadcasted_iota(jnp.int32, (size, size), 0)
    lanef = lane.astype(f32)
    for c in range(cols):
        hit = lanef == mirrors[:, c : c + 1]
        tile = jnp.where(hit, gains[:, c : c + 1], 0.0)
        other = jnp.where(owner[c] == c, 0.0, 1.0)
        ghosts[c] = jnp.where(eye, tile * other, tile)

    has_south = lax.axis_index("slab") < lax.axis_size("slab") - 1
    has_west = lax.axis_index("cross") > 0
    has_east = lax.axis_index("cross") < lax.axis_size("cross") - 1
    sums = jnp.zeros((size, size), f32)
    for r in range(rows):
        part = pl.ds(r * cols, cols)
        pltpu.make_async_copy(self_hbm.at[part], self_in.at[part], self_sem.at[r]).wait()
        part = pl.ds(r * cols * slots, cols * slots)
        pltpu.make_async_copy(edge_hbm.at[part], edge_in.at[part], edge_sem.at[r]).wait()
        for c in range(cols):
            block = r * cols + c
            at = r * STRIDE + c + 1
            tile = jnp.where(eye, 0.0, self_in[block])
            rowwise = tile
            v_out[at : at + 1, :] += jnp.sum(tile, axis=0, keepdims=True)
            for k in range(slots):
                code = offset[r, c, k]
                live = jnp.where(k < count[r, c], 1.0, 0.0)
                there = jnp.asarray(True)
                if c == 0:
                    there = there & (has_west | (code != 1))
                if c == cols - 1:
                    there = there & (has_east | ((code != 0) & (code != 3)))
                if r == rows - 1:
                    there = there & (has_south | (code == 0))
                tile = edge_in[block * slots + k]
                rowwise += tile * jnp.where(there, live, 0.0)
                step = jnp.where(code == 0, CODE_STEP[0], CODE_STEP[1] - 1 + code)
                v_out[pl.ds(at + step, 1), :] += jnp.sum(tile, axis=0, keepdims=True) * live
            if r == rows - 1:
                tile = ghosts[c]
                rowwise += tile
                j = r * STRIDE + 1 + owner[c]
                v_out[pl.ds(j, 1), :] += jnp.sum(tile, axis=0, keepdims=True)
            sums = jnp.where(lane == at, jnp.sum(rowwise, axis=1, keepdims=True), sums)
    v_out[...] += jnp.transpose(sums)[: v_out.shape[0], :]
    pack_sides(v_out, first, second, rows, cols)


def place_kernel(
    rows, cols, count, offset, owner, self_in, edge_in, mask, selfs, edges
):
    size = mask.shape[1]
    slots = len(CODE_STEP)
    lane = lax.broadcasted_iota(jnp.int32, (size, size), 1)
    eye = lane == lax.broadcasted_iota(jnp.int32, (size, size), 0)
    for r in range(rows):
        for c in range(cols):
            block = r * cols + c
            selfs[block] = jnp.where(eye, 0.0, self_in[block])
            for k in range(slots):
                place = block * slots + offset[r, c, k]
                live = jnp.where(k < count[r, c], 1.0, 0.0)
                mask[pl.ds(place, 1), :] = jnp.full((1, size), live, f32)
                edges[place] = edge_in[block * slots + k]
    base = rows * cols * slots
    for c in range(cols):
        for o in range(cols):
            same = jnp.where(owner[c] == o, 1.0, 0.0)
            mask[base + c * cols + o : base + c * cols + o + 1, :] = jnp.full((1, size), same, f32)


def add_rims(rows, total, first, second, out):
    even = on_even("slab")
    has_north = lax.axis_index("slab") > 0
    out[...] = total[...]
    north = jnp.where(even, second[:STRIDE, :], first[:STRIDE, :])
    out[:STRIDE, :] += jnp.where(has_north, north, 0.0)
    out[rows * STRIDE :, :] += jnp.where(even, first[:STRIDE, :], second[:STRIDE, :])


def early_kernel(rows, cols, sign, mask, selfs, edges, ghosts, top, bottom, v_out, p_ref):
    inside, _ = inside_grid(rows, cols, v_out.shape)
    at = lax.broadcasted_iota(jnp.int32, v_out.shape, 0)
    known = inside & (at >= STRIDE) & (at < rows * STRIDE)
    field = jnp.where(known, top[...] / jnp.where(known, sign * bottom[...], 1.0), 0.0)
    p_ref[...] = jnp.zeros_like(p_ref)
    p_ref[: field.shape[0], :] = field
    v_out[...] = jnp.zeros_like(v_out)
    tiles = Tiles(rows, cols, p_ref, mask, selfs, edges, ghosts)
    tiles.early()
    tiles.store(v_out)


def second_kernel(
    rows, cols, mask, selfs, edges, ghosts, early, total, src, rim1, rim2,
    v_out, s_out, jac_out, side1, side2, p_ref,
):
    inside, _ = inside_grid(rows, cols, v_out.shape)
    add_rims(rows, total, rim1, rim2, jac_out)
    s_out[...] = src[...]
    s_out[rows * STRIDE :, :] = jnp.where(
        on_even("slab"), rim1[STRIDE:, :], rim2[STRIDE:, :]
    )
    jac = jnp.where(inside, -jac_out[...], 1.0)
    s = jnp.where(inside, s_out[...] / jac, 0.0)
    p_ref[...] = jnp.zeros_like(p_ref)
    p_ref[: s.shape[0], :] = s
    s_out[...] = s
    jac_out[...] = jac
    v_out[...] = early[...]
    tiles = Tiles(rows, cols, p_ref, mask, selfs, edges, ghosts)
    tiles.late()
    tiles.store(v_out)
    for side in (side1, side2):
        side[...] = jnp.zeros_like(side)
    pack_sides(v_out, side1, side2, rows, cols)


def third_kernel(
    rows, cols, mask, selfs, edges, ghosts, early, total, src, s_ref, jac, rim1, rim2,
    v_out, w_out, side1, side2, sums_out, p_ref,
):
    size = p_ref.shape[1]
    inside, own = inside_grid(rows, cols, v_out.shape)
    add_rims(rows, total, rim1, rim2, w_out)
    u = w_out[...]
    w = jnp.where(inside, u / jac[...], 0.0)
    p_ref[...] = jnp.zeros_like(p_ref)
    p_ref[: w.shape[0], :] = w
    w_out[...] = w
    v_out[...] = early[...]
    tiles = Tiles(rows, cols, p_ref, mask, selfs, edges, ghosts)
    tiles.late()
    tiles.store(v_out)
    for side in (side1, side2):
        side[...] = jnp.zeros_like(side)
    pack_sides(v_out, side1, side2, rows, cols)
    s = s_ref[...]

    def whole(x):
        return jnp.sum(jnp.sum(x, axis=0, keepdims=True), axis=1, keepdims=True)

    sums = (
        whole(jnp.where(own, src[...] * s, 0.0)),
        whole(jnp.where(own, s * u, 0.0)),
        whole(jnp.where(own, w * u, 0.0)),
        whole(w * v_out[...]),
    )
    lane = lax.broadcasted_iota(jnp.int32, (1, size), 1)
    line = jnp.zeros((1, size), f32)
    for k, value in enumerate(sums):
        line = jnp.where(lane == k, value, line)
    sums_out[...] = jnp.broadcast_to(line, sums_out.shape)


def merge_kernel(rows, cols, with_src, *refs):
    v, side1, side2 = refs[:3]
    total, first, second = refs[3 + with_src : 6 + with_src]
    even = on_even("cross")
    has_west = lax.axis_index("cross") > 0
    has_east = lax.axis_index("cross") < lax.axis_size("cross") - 1
    west = jnp.where(even, side2[...], side1[...])
    east = jnp.where(even, side1[...], side2[...])
    west = jnp.where(has_west, west, 0.0)
    east = jnp.where(has_east, east, 0.0)
    total[...] = v[...]
    for r in range(rows + 1):
        lo = r * STRIDE
        total[lo : lo + 2, :] += west[2 * r : 2 * r + 2, :]
        total[lo + cols : lo + cols + 2, :] += east[2 * r : 2 * r + 2, :]
    top, bottom = total[:STRIDE, :], total[rows * STRIDE :, :]
    even = on_even("slab")
    first[:STRIDE, :] = jnp.where(even, bottom, top)
    second[:STRIDE, :] = jnp.where(even, top, bottom)
    if with_src:
        src, src_out = refs[3], refs[7]
        src_out[...] = src[...]
        for r in range(rows):
            lo, head = r * STRIDE, 2 * (rows + 1) + r
            src_out[lo : lo + 1, :] = west[head : head + 1, :]
            src_out[lo + cols + 1 : lo + cols + 2, :] = east[head : head + 1, :]
        for out in (first, second):
            out[STRIDE:, :] = src_out[:STRIDE, :]


def last_kernel(
    rows, cols, gathered, total, rim1, rim2, s_ref, jac_ref, w_ref, pressure, residual, v
):
    add_rims(rows, total, rim1, rim2, v)
    nu = jnp.sum(gathered[...], axis=0, keepdims=True)
    nu0, nu1, nu2, nu3 = (nu[:, k : k + 1] for k in range(4))
    rho = nu1 / nu0
    a0 = 1.0 / (1.0 + rho)
    norm1 = a0 * a0 * (nu2 - rho * nu1)
    beta = norm1 / nu0
    g = a0 * rho + beta
    cross = g * g * nu1 - 2.0 * g * a0 * nu2 + a0 * a0 * nu3
    sigma = jnp.where(norm1 > 0.0, beta + cross / norm1, 0.0)
    step = 1.0 / (1.0 + sigma)
    rest = sigma * step
    ps, pw = a0 + step * g, -step * a0
    rs, rw, rv = a0 * rho * rest - step * beta, -a0 * rest - step * g, step * a0
    for r in range(rows):
        lo = r * STRIDE + 1
        s, w, jac = s_ref[lo : lo + cols, :], w_ref[lo : lo + cols, :], jac_ref[lo : lo + cols, :]
        pressure[r] = ps * s + pw * w
        residual[r] = jac * (rs * s + rw * w) + rv * v[lo : lo + cols, :]


def swap(value, second, axis):
    slabs, crosses = lax.axis_size("slab"), lax.axis_size("cross")
    pairs = []
    for a in range(slabs):
        for c in range(crosses):
            if axis == "cross":
                to = (a, (((c + 1) ^ 1) - 1) % crosses if second else c ^ 1)
            elif not second:
                to = (a ^ 1, c)
            elif 0 < a < slabs - 1:
                to = (((a + 1) ^ 1) - 1, c)
            else:
                to = (a, c ^ 1)
            pairs.append((a * crosses + c, to[0] * crosses + to[1]))
    return lax.ppermute(value, ("slab", "cross"), pairs)


def per_device(
    velocity,
    acceleration,
    grad_coef,
    density_dev,
    self_weight,
    self_tiles,
    edge_tiles,
    tile_count,
    tile_offset,
    ghost_owner,
    ghost_mirror,
    ghost_gain,
):
    rows, cols, size = self_weight.shape
    slots = tile_offset.shape[-1]
    region = ((rows + 1) * STRIDE, size)
    side = (STRIDE * pl.cdiv(2 * (rows + 1) + rows, STRIDE), size)
    line = (STRIDE, size)
    peers = lax.axis_size("slab") * lax.axis_size("cross")

    def call(kernel, shapes, specs, operands, scratch=(), extra=(), limit=2):
        return pl.pallas_call(
            functools.partial(kernel, rows, cols, *extra),
            out_shape=[pltpu.VMEM(shape, f32) for shape in shapes],
            in_specs=specs,
            out_specs=[VMEM] * len(shapes),
            scratch_shapes=list(scratch),
            compiler_params=pltpu.CompilerParams(vmem_limit_bytes=limit << 20),
        )(*operands)

    def exchange(v, first, second, src=None):
        first = swap(first, False, "cross")
        second = swap(second, True, "cross")
        operands = [v, first, second]
        shapes = [region, line, line]
        if src is not None:
            operands.append(src)
            shapes = [region, (2 * STRIDE, size), (2 * STRIDE, size), region]
        total, first, second, *rest = call(
            merge_kernel, shapes, [VMEM] * len(operands), operands, extra=(src is not None,)
        )
        first = swap(first, False, "slab")
        second = swap(second, True, "slab")
        return [total, *rest, first, second]

    def early(top, bottom, sign):
        operands = matrix + [top, bottom]
        return call(early_kernel, [region], [VMEM] * len(operands), operands, [field], (sign,))[0]

    field = pltpu.VMEM((size, size), f32)
    small = [
        tile_count, tile_offset, ghost_owner, ghost_mirror, ghost_gain,
        velocity, acceleration, grad_coef, density_dev, self_weight,
    ]
    staged = [
        (pltpu.SMEM if k < 3 else pltpu.VMEM)(x.shape, x.dtype) for k, x in enumerate(small)
    ]
    v, src, first, second, self_in, edge_in, ghosts = call(
        first_kernel,
        [
            region, region, side, side,
            (rows * cols, size, size), (rows * cols * slots, size, size), (cols, size, size),
        ],
        [HBM] * 12,
        [
            pltpu.with_memory_space_constraint(x, pltpu.HBM)
            for x in small
            + [
                self_tiles.reshape(rows * cols, size, size),
                edge_tiles.reshape(rows * cols * slots, size, size),
            ]
        ],
        staged + [pltpu.SemaphoreType.DMA((n,)) for n in (len(small), rows, rows)],
        limit=10,
    )
    matrix = [*call(
        place_kernel,
        [
            (rows * cols * slots + cols * cols, size),
            (rows * cols, size, size), (rows * cols * slots, size, size),
        ],
        [SMEM] * 3 + [VMEM] * 2,
        small[:3] + [self_in, edge_in],
    ), ghosts]
    total, src, rim1, rim2 = exchange(v, first, second, src)
    part = early(src, total, -1.0)

    operands = matrix + [part, total, src, rim1, rim2]
    v, s, jac, first, second = call(
        second_kernel, [region] * 3 + [side] * 2, [VMEM] * len(operands), operands, [field]
    )
    total, rim1, rim2 = exchange(v, first, second)
    part = early(total, jac, 1.0)

    operands = matrix + [part, total, src, s, jac, rim1, rim2]
    v, w, first, second, sums = call(
        third_kernel,
        [region] * 2 + [side] * 2 + [(peers, size)],
        [VMEM] * len(operands), operands, [field],
    )
    gathered = lax.all_to_all(sums, ("slab", "cross"), 0, 0, tiled=True)
    total, rim1, rim2 = exchange(v, first, second)

    return tuple(
        pl.pallas_call(
            functools.partial(last_kernel, rows, cols),
            out_shape=[jax.ShapeDtypeStruct((rows, cols, size), f32)] * 2,
            in_specs=[VMEM] * 7,
            out_specs=[VMEM] * 2,
            scratch_shapes=[pltpu.VMEM(region, f32)],
            compiler_params=pltpu.CompilerParams(vmem_limit_bytes=2 << 20),
        )(gathered, total, rim1, rim2, s, jac, w)
    )


def solution(mesh):
    in_specs = (
        P(None, "slab", "cross", None),
        P(None, "slab", "cross", None),
        P(None, "slab", "cross", None),
        P("slab", "cross", None),
        P("slab", "cross", None),
        P("slab", "cross", None, None),
        P("slab", "cross", None, None, None),
        P("slab", "cross"),
        P("slab", "cross", None),
        P("cross"),
        P("cross", None),
        P("cross", None),
    )
    out_specs = (P("slab", "cross", None), P("slab", "cross", None))
    return jax.shard_map(
        per_device, mesh=mesh, in_specs=in_specs, out_specs=out_specs, check_vma=False
    )
```

```python
import functools

import jax
import jax.numpy as jnp
from jax import lax
from jax.experimental import pallas as pl
from jax.experimental.pallas import tpu as pltpu
from jax.sharding import PartitionSpec as P


STRIDE = 8
CODE_STEP = (1, STRIDE - 1, STRIDE, STRIDE + 1)

VMEM = pl.BlockSpec(memory_space=pltpu.VMEM)
SMEM = pl.BlockSpec(memory_space=pltpu.SMEM)
HBM = pl.BlockSpec(memory_space=pltpu.HBM)
f32 = jnp.float32


def inside_grid(rows, cols, shape):
    slab, cross = lax.axis_index("slab"), lax.axis_index("cross")
    has_south = slab < lax.axis_size("slab") - 1
    at = lax.broadcasted_iota(jnp.int32, shape, 0)
    column = at % STRIDE
    first = jnp.where(cross > 0, 0, 1)
    last = jnp.where(cross < lax.axis_size("cross") - 1, cols + 1, cols)
    end = jnp.where(has_south, rows + 1, rows) * STRIDE
    own = (at < rows * STRIDE) & (column >= 1) & (column <= cols)
    return (column >= first) & (column <= last) & (at < end), own


class Tiles:
    def __init__(self, rows, cols, p_ref, mask, selfs, edges, ghosts):
        self.rows, self.cols, self.p_ref, self.mask = rows, cols, p_ref, mask
        self.selfs, self.edges, self.ghosts = selfs, edges, ghosts
        self.size = p_ref.shape[1]
        full = (self.size, self.size)
        self.lane = lax.broadcasted_iota(jnp.int32, full, 1)
        self.columns = jnp.transpose(p_ref[...])
        self.sums = jnp.zeros(full, f32)
        self.parts = {}

    def fold(self, product, at, factor=None):
        part = jnp.sum(product.reshape(self.size // 8, 8, self.size), axis=0)
        if factor is not None:
            part = part * factor
        self.parts[at] = self.parts[at] + part if at in self.parts else part

    def block(self, r, c, codes=(0, 1, 2, 3), local=True):
        size, cols = self.size, self.cols
        at = r * STRIDE + c + 1
        down = jnp.broadcast_to(self.columns[:, at : at + 1], (size, size))
        acc = None
        if local:
            tile = self.selfs[r * cols + c]
            acc = tile * self.p_ref[at : at + 1, :]
            self.fold(tile * down, at)
        for code in codes:
            slot = (r * cols + c) * len(CODE_STEP) + code
            live = self.mask[slot : slot + 1, :]
            j = at + CODE_STEP[code]
            tile = self.edges[slot]
            product = tile * (self.p_ref[j : j + 1, :] * live)
            acc = product if acc is None else acc + product
            self.fold(tile * down, j, live)
        if local and r == self.rows - 1:
            tile = self.ghosts[c]
            base = self.rows * cols * len(CODE_STEP) + c * cols
            field = jnp.zeros((1, size), f32)
            for o in range(cols):
                j = r * STRIDE + 1 + o
                field += self.p_ref[j : j + 1, :] * self.mask[base + o : base + o + 1, :]
            acc += tile * field
            product = tile * down
            for o in range(cols):
                self.fold(product, r * STRIDE + 1 + o, self.mask[base + o : base + o + 1, :])
        self.sums = jnp.where(self.lane == at, jnp.sum(acc, axis=1, keepdims=True), self.sums)

    def early(self):
        for r in range(1, self.rows):
            for c in range(self.cols):
                self.block(r, c, (0, 1, 2, 3) if r < self.rows - 1 else (0,))

    def late(self):
        for c in range(self.cols):
            self.block(0, c)
        for c in range(self.cols):
            self.block(self.rows - 1, c, (1, 2, 3), False)

    def store(self, v_ref):
        v_ref[...] += jnp.transpose(self.sums)[: v_ref.shape[0], :]
        for at, part in self.parts.items():
            v_ref[at : at + 1, :] += jnp.sum(part, axis=0, keepdims=True)


def on_even(axis):
    return lax.axis_index(axis) % 2 == 0


def pack_sides(v_ref, first, second, rows, cols):
    even = on_even("cross")
    for r in range(rows + 1):
        east = v_ref[r * STRIDE + cols : r * STRIDE + cols + 2, :]
        west = v_ref[r * STRIDE : r * STRIDE + 2, :]
        first[2 * r : 2 * r + 2, :] = jnp.where(even, east, west)
        second[2 * r : 2 * r + 2, :] = jnp.where(even, west, east)


def first_kernel(rows, cols, *refs):
    inputs, refs = refs[:12], refs[12:]
    (v_out, src_out, first, second, self_in, edge_in, ghosts), refs = refs[:7], refs[7:]
    staged, (small_sem, self_sem, edge_sem) = refs[:10], refs[10:]
    self_hbm, edge_hbm = inputs[10:]
    size = v_out.shape[1]
    slots = len(CODE_STEP)
    small = [
        pltpu.make_async_copy(hbm, here, small_sem.at[k])
        for k, (hbm, here) in enumerate(zip(inputs[:10], staged))
    ]
    for copy in small:
        copy.start()
    for r in range(rows):
        part = pl.ds(r * cols, cols)
        pltpu.make_async_copy(self_hbm.at[part], self_in.at[part], self_sem.at[r]).start()
    for r in range(rows):
        for h in range(2):
            part = pl.ds((2 * r + h) * cols * slots // 2, cols * slots // 2)
            pltpu.make_async_copy(
                edge_hbm.at[part], edge_in.at[part], edge_sem.at[2 * r + h]
            ).start()
    count, offset, owner, mirror, gain, vel, acc, grad, dens, weight = staged
    for copy in small:
        copy.wait()
    v_out[...] = jnp.zeros_like(v_out)
    src_out[...] = jnp.zeros_like(src_out)
    even = on_even("cross")
    for r in range(rows):
        lo = r * STRIDE + 1
        total = jnp.zeros((cols, size), f32)
        for d in range(3):
            total += grad[d, r] * (vel[d, r] + 0.5 * acc[d, r])
        src = dens[r] / 0.25 - total / 0.5
        src_out[lo : lo + cols, :] = src
        v_out[lo : lo + cols, :] = -weight[r]
        head = 2 * (rows + 1) + r
        east, west = src[cols - 1 : cols, :], src[0:1, :]
        first[head : head + 1, :] = jnp.where(even, east, west)
        second[head : head + 1, :] = jnp.where(even, west, east)
    for side in (first, second):
        for row in range(2 * (rows + 1) + rows, side.shape[0]):
            side[row : row + 1, :] = jnp.zeros((1, size), f32)

    on_wall = lax.axis_index("slab") == lax.axis_size("slab") - 1
    pad = jnp.zeros((size - cols, size), f32)
    mirrors = jnp.transpose(jnp.concatenate([mirror[...].astype(f32), pad], axis=0))
    gains = jnp.transpose(
        jnp.concatenate([gain[...] * jnp.where(on_wall, -1.0, 0.0), pad], axis=0)
    )
    lane = lax.broadcasted_iota(jnp.int32, (size, size), 1)
    eye = lane == lax.broadcasted_iota(jnp.int32, (size, size), 0)
    lanef = lane.astype(f32)
    for c in range(cols):
        hit = lanef == mirrors[:, c : c + 1]
        tile = jnp.where(hit, gains[:, c : c + 1], 0.0)
        other = jnp.where(owner[c] == c, 0.0, 1.0)
        ghosts[c] = jnp.where(eye, tile * other, tile)

    has_south = lax.axis_index("slab") < lax.axis_size("slab") - 1
    has_west = lax.axis_index("cross") > 0
    has_east = lax.axis_index("cross") < lax.axis_size("cross") - 1
    sums = jnp.zeros((size, size), f32)
    for r in range(rows):
        part = pl.ds(r * cols, cols)
        pltpu.make_async_copy(self_hbm.at[part], self_in.at[part], self_sem.at[r]).wait()
        for c in range(cols):
            if c % 2 == 0:
                h = 2 * c // cols
                part = pl.ds((2 * r + h) * cols * slots // 2, cols * slots // 2)
                pltpu.make_async_copy(
                    edge_hbm.at[part], edge_in.at[part], edge_sem.at[2 * r + h]
                ).wait()
            block = r * cols + c
            at = r * STRIDE + c + 1
            tile = jnp.where(eye, 0.0, self_in[block])
            rowwise = tile
            v_out[at : at + 1, :] += jnp.sum(tile, axis=0, keepdims=True)
            for k in range(slots):
                code = offset[r, c, k]
                live = jnp.where(k < count[r, c], 1.0, 0.0)
                there = jnp.asarray(True)
                if c == 0:
                    there = there & (has_west | (code != 1))
                if c == cols - 1:
                    there = there & (has_east | ((code != 0) & (code != 3)))
                if r == rows - 1:
                    there = there & (has_south | (code == 0))
                tile = edge_in[block * slots + k]
                rowwise += tile * jnp.where(there, live, 0.0)
                step = jnp.where(code == 0, CODE_STEP[0], CODE_STEP[1] - 1 + code)
                v_out[pl.ds(at + step, 1), :] += jnp.sum(tile, axis=0, keepdims=True) * live
            if r == rows - 1:
                tile = ghosts[c]
                rowwise += tile
                j = r * STRIDE + 1 + owner[c]
                v_out[pl.ds(j, 1), :] += jnp.sum(tile, axis=0, keepdims=True)
            sums = jnp.where(lane == at, jnp.sum(rowwise, axis=1, keepdims=True), sums)
    v_out[...] += jnp.transpose(sums)[: v_out.shape[0], :]
    pack_sides(v_out, first, second, rows, cols)


def place_kernel(
    rows, cols, count, offset, owner, self_in, edge_in, mask, selfs, edges
):
    size = mask.shape[1]
    slots = len(CODE_STEP)
    lane = lax.broadcasted_iota(jnp.int32, (size, size), 1)
    eye = lane == lax.broadcasted_iota(jnp.int32, (size, size), 0)
    for r in range(rows):
        for c in range(cols):
            block = r * cols + c
            selfs[block] = jnp.where(eye, 0.0, self_in[block])
            for k in range(slots):
                place = block * slots + offset[r, c, k]
                live = jnp.where(k < count[r, c], 1.0, 0.0)
                mask[pl.ds(place, 1), :] = jnp.full((1, size), live, f32)
                edges[place] = edge_in[block * slots + k]
    base = rows * cols * slots
    for c in range(cols):
        for o in range(cols):
            same = jnp.where(owner[c] == o, 1.0, 0.0)
            mask[base + c * cols + o : base + c * cols + o + 1, :] = jnp.full((1, size), same, f32)


def add_rims(rows, total, first, second, out):
    even = on_even("slab")
    has_north = lax.axis_index("slab") > 0
    out[...] = total[...]
    north = jnp.where(even, second[:STRIDE, :], first[:STRIDE, :])
    out[:STRIDE, :] += jnp.where(has_north, north, 0.0)
    out[rows * STRIDE :, :] += jnp.where(even, first[:STRIDE, :], second[:STRIDE, :])


def early_kernel(rows, cols, sign, mask, selfs, edges, ghosts, top, bottom, v_out, p_ref):
    inside, _ = inside_grid(rows, cols, v_out.shape)
    at = lax.broadcasted_iota(jnp.int32, v_out.shape, 0)
    known = inside & (at >= STRIDE) & (at < rows * STRIDE)
    field = jnp.where(known, top[...] / jnp.where(known, sign * bottom[...], 1.0), 0.0)
    p_ref[...] = jnp.zeros_like(p_ref)
    p_ref[: field.shape[0], :] = field
    v_out[...] = jnp.zeros_like(v_out)
    tiles = Tiles(rows, cols, p_ref, mask, selfs, edges, ghosts)
    tiles.early()
    tiles.store(v_out)


def second_kernel(
    rows, cols, mask, selfs, edges, ghosts, early, total, src, rim1, rim2,
    v_out, s_out, jac_out, side1, side2, p_ref,
):
    inside, _ = inside_grid(rows, cols, v_out.shape)
    add_rims(rows, total, rim1, rim2, jac_out)
    s_out[...] = src[...]
    s_out[rows * STRIDE :, :] = jnp.where(
        on_even("slab"), rim1[STRIDE:, :], rim2[STRIDE:, :]
    )
    jac = jnp.where(inside, -jac_out[...], 1.0)
    s = jnp.where(inside, s_out[...] / jac, 0.0)
    p_ref[...] = jnp.zeros_like(p_ref)
    p_ref[: s.shape[0], :] = s
    s_out[...] = s
    jac_out[...] = jac
    v_out[...] = early[...]
    tiles = Tiles(rows, cols, p_ref, mask, selfs, edges, ghosts)
    tiles.late()
    tiles.store(v_out)
    for side in (side1, side2):
        side[...] = jnp.zeros_like(side)
    pack_sides(v_out, side1, side2, rows, cols)


def third_kernel(
    rows, cols, mask, selfs, edges, ghosts, early, total, src, s_ref, jac, rim1, rim2,
    v_out, w_out, side1, side2, sums_out, p_ref,
):
    size = p_ref.shape[1]
    inside, own = inside_grid(rows, cols, v_out.shape)
    add_rims(rows, total, rim1, rim2, w_out)
    u = w_out[...]
    w = jnp.where(inside, u / jac[...], 0.0)
    p_ref[...] = jnp.zeros_like(p_ref)
    p_ref[: w.shape[0], :] = w
    w_out[...] = w
    v_out[...] = early[...]
    tiles = Tiles(rows, cols, p_ref, mask, selfs, edges, ghosts)
    tiles.late()
    tiles.store(v_out)
    for side in (side1, side2):
        side[...] = jnp.zeros_like(side)
    pack_sides(v_out, side1, side2, rows, cols)
    s = s_ref[...]

    def whole(x):
        return jnp.sum(jnp.sum(x, axis=0, keepdims=True), axis=1, keepdims=True)

    sums = (
        whole(jnp.where(own, src[...] * s, 0.0)),
        whole(jnp.where(own, s * u, 0.0)),
        whole(jnp.where(own, w * u, 0.0)),
        whole(w * v_out[...]),
    )
    lane = lax.broadcasted_iota(jnp.int32, (1, size), 1)
    line = jnp.zeros((1, size), f32)
    for k, value in enumerate(sums):
        line = jnp.where(lane == k, value, line)
    sums_out[...] = jnp.broadcast_to(line, sums_out.shape)


def merge_kernel(rows, cols, with_src, *refs):
    v, side1, side2 = refs[:3]
    total, first, second = refs[3 + with_src : 6 + with_src]
    even = on_even("cross")
    has_west = lax.axis_index("cross") > 0
    has_east = lax.axis_index("cross") < lax.axis_size("cross") - 1
    west = jnp.where(even, side2[...], side1[...])
    east = jnp.where(even, side1[...], side2[...])
    west = jnp.where(has_west, west, 0.0)
    east = jnp.where(has_east, east, 0.0)
    total[...] = v[...]
    for r in range(rows + 1):
        lo = r * STRIDE
        total[lo : lo + 2, :] += west[2 * r : 2 * r + 2, :]
        total[lo + cols : lo + cols + 2, :] += east[2 * r : 2 * r + 2, :]
    top, bottom = total[:STRIDE, :], total[rows * STRIDE :, :]
    even = on_even("slab")
    first[:STRIDE, :] = jnp.where(even, bottom, top)
    second[:STRIDE, :] = jnp.where(even, top, bottom)
    if with_src:
        src, src_out = refs[3], refs[7]
        src_out[...] = src[...]
        for r in range(rows):
            lo, head = r * STRIDE, 2 * (rows + 1) + r
            src_out[lo : lo + 1, :] = west[head : head + 1, :]
            src_out[lo + cols + 1 : lo + cols + 2, :] = east[head : head + 1, :]
        for out in (first, second):
            out[STRIDE:, :] = src_out[:STRIDE, :]


def last_kernel(
    rows, cols, gathered, total, rim1, rim2, s_ref, jac_ref, w_ref, pressure, residual, v
):
    add_rims(rows, total, rim1, rim2, v)
    nu = jnp.sum(gathered[...], axis=0, keepdims=True)
    nu0, nu1, nu2, nu3 = (nu[:, k : k + 1] for k in range(4))
    rho = nu1 / nu0
    a0 = 1.0 / (1.0 + rho)
    norm1 = a0 * a0 * (nu2 - rho * nu1)
    beta = norm1 / nu0
    g = a0 * rho + beta
    cross = g * g * nu1 - 2.0 * g * a0 * nu2 + a0 * a0 * nu3
    sigma = jnp.where(norm1 > 0.0, beta + cross / norm1, 0.0)
    step = 1.0 / (1.0 + sigma)
    rest = sigma * step
    ps, pw = a0 + step * g, -step * a0
    rs, rw, rv = a0 * rho * rest - step * beta, -a0 * rest - step * g, step * a0
    for r in range(rows):
        lo = r * STRIDE + 1
        s, w, jac = s_ref[lo : lo + cols, :], w_ref[lo : lo + cols, :], jac_ref[lo : lo + cols, :]
        pressure[r] = ps * s + pw * w
        residual[r] = jac * (rs * s + rw * w) + rv * v[lo : lo + cols, :]


def swap(value, second, axis):
    slabs, crosses = lax.axis_size("slab"), lax.axis_size("cross")
    pairs = []
    for a in range(slabs):
        for c in range(crosses):
            if axis == "cross":
                to = (a, (((c + 1) ^ 1) - 1) % crosses if second else c ^ 1)
            elif not second:
                to = (a ^ 1, c)
            elif 0 < a < slabs - 1:
                to = (((a + 1) ^ 1) - 1, c)
            else:
                to = (a, c ^ 1)
            pairs.append((a * crosses + c, to[0] * crosses + to[1]))
    return lax.ppermute(value, ("slab", "cross"), pairs)


def per_device(
    velocity,
    acceleration,
    grad_coef,
    density_dev,
    self_weight,
    self_tiles,
    edge_tiles,
    tile_count,
    tile_offset,
    ghost_owner,
    ghost_mirror,
    ghost_gain,
):
    rows, cols, size = self_weight.shape
    slots = tile_offset.shape[-1]
    region = ((rows + 1) * STRIDE, size)
    side = (STRIDE * pl.cdiv(2 * (rows + 1) + rows, STRIDE), size)
    line = (STRIDE, size)
    peers = lax.axis_size("slab") * lax.axis_size("cross")

    def call(kernel, shapes, specs, operands, scratch=(), extra=(), limit=2):
        return pl.pallas_call(
            functools.partial(kernel, rows, cols, *extra),
            out_shape=[pltpu.VMEM(shape, f32) for shape in shapes],
            in_specs=specs,
            out_specs=[VMEM] * len(shapes),
            scratch_shapes=list(scratch),
            compiler_params=pltpu.CompilerParams(vmem_limit_bytes=limit << 20),
        )(*operands)

    def exchange(v, first, second, src=None):
        first = swap(first, False, "cross")
        second = swap(second, True, "cross")
        operands = [v, first, second]
        shapes = [region, line, line]
        if src is not None:
            operands.append(src)
            shapes = [region, (2 * STRIDE, size), (2 * STRIDE, size), region]
        total, first, second, *rest = call(
            merge_kernel, shapes, [VMEM] * len(operands), operands, extra=(src is not None,)
        )
        first = swap(first, False, "slab")
        second = swap(second, True, "slab")
        return [total, *rest, first, second]

    def early(top, bottom, sign):
        operands = matrix + [top, bottom]
        return call(early_kernel, [region], [VMEM] * len(operands), operands, [field], (sign,))[0]

    field = pltpu.VMEM((size, size), f32)
    small = [
        tile_count, tile_offset, ghost_owner, ghost_mirror, ghost_gain,
        velocity, acceleration, grad_coef, density_dev, self_weight,
    ]
    staged = [
        (pltpu.SMEM if k < 3 else pltpu.VMEM)(x.shape, x.dtype) for k, x in enumerate(small)
    ]
    v, src, first, second, self_in, edge_in, ghosts = call(
        first_kernel,
        [
            region, region, side, side,
            (rows * cols, size, size), (rows * cols * slots, size, size), (cols, size, size),
        ],
        [HBM] * 12,
        [
            pltpu.with_memory_space_constraint(x, pltpu.HBM)
            for x in small
            + [
                self_tiles.reshape(rows * cols, size, size),
                edge_tiles.reshape(rows * cols * slots, size, size),
            ]
        ],
        staged + [pltpu.SemaphoreType.DMA((n,)) for n in (len(small), rows, 2 * rows)],
        limit=10,
    )
    matrix = [*call(
        place_kernel,
        [
            (rows * cols * slots + cols * cols, size),
            (rows * cols, size, size), (rows * cols * slots, size, size),
        ],
        [SMEM] * 3 + [VMEM] * 2,
        small[:3] + [self_in, edge_in],
    ), ghosts]
    total, src, rim1, rim2 = exchange(v, first, second, src)
    part = early(src, total, -1.0)

    operands = matrix + [part, total, src, rim1, rim2]
    v, s, jac, first, second = call(
        second_kernel, [region] * 3 + [side] * 2, [VMEM] * len(operands), operands, [field]
    )
    total, rim1, rim2 = exchange(v, first, second)
    part = early(total, jac, 1.0)

    operands = matrix + [part, total, src, s, jac, rim1, rim2]
    v, w, first, second, sums = call(
        third_kernel,
        [region] * 2 + [side] * 2 + [(peers, size)],
        [VMEM] * len(operands), operands, [field],
    )
    gathered = lax.all_to_all(sums, ("slab", "cross"), 0, 0, tiled=True)
    total, rim1, rim2 = exchange(v, first, second)

    return tuple(
        pl.pallas_call(
            functools.partial(last_kernel, rows, cols),
            out_shape=[jax.ShapeDtypeStruct((rows, cols, size), f32)] * 2,
            in_specs=[VMEM] * 7,
            out_specs=[VMEM] * 2,
            scratch_shapes=[pltpu.VMEM(region, f32)],
            compiler_params=pltpu.CompilerParams(vmem_limit_bytes=2 << 20),
        )(gathered, total, rim1, rim2, s, jac, w)
    )


def solution(mesh):
    in_specs = (
        P(None, "slab", "cross", None),
        P(None, "slab", "cross", None),
        P(None, "slab", "cross", None),
        P("slab", "cross", None),
        P("slab", "cross", None),
        P("slab", "cross", None, None),
        P("slab", "cross", None, None, None),
        P("slab", "cross"),
        P("slab", "cross", None),
        P("cross"),
        P("cross", None),
        P("cross", None),
    )
    out_specs = (P("slab", "cross", None), P("slab", "cross", None))
    return jax.shard_map(
        per_device, mesh=mesh, in_specs=in_specs, out_specs=out_specs, check_vma=False
    )
```
